32 devices in a mesh: img: 2 (over x), sub: 16 (over z, y, core).
Axes of the slice: x: 2, y: 2, z: 4, core: 2. Of those that a mesh axis runs over, the one named last changes fastest.
Arguments:
- sub_images: float32 [2, 512, 4096], P(None, ('img', 'sub')), parts along dimension 1, may hold values from -6 to 6
- shift_table: int32 [4, 16, 2, 8], P(None, 'sub'), may hold values from -256 to 256
- phase_table: float32 [4, 16, 2, 8], P(None, 'sub'), may hold values from -3.140625 to 3.140625
- offset_table: int32 [4, 16, 2, 16], P(None, 'sub'), may hold values from 0 to 4
- weight_table: float32 [4, 16, 2, 4, 16], P(None, 'sub'), may hold values from -2 to 2
Outputs:
- turned_image: float32 [2, 8192, 256], P(None, ('img', 'sub')), parts along dimension 1
The draws below stay inside these ranges and needn't reach their ends.
There are 2 independent parts, one for each index of `img`. The reference program is written for one: setup_inputs(seed, part) draws one part's arguments, and reference() takes and returns one part's arrays. A program takes and returns all parts, laid end to end along the dimension named above; an argument that names none is the same for every part. Nothing has to cross between parts.
All inputs are finite; a program needn't handle non-finite values.
Results may differ from the reference program's by a relative error of at most 0.0003.
Values sent between devices are 32-bit elements; how exact they have to be, the bound alone decides.
No kernel may reach another device: no remote copies, remote signals or barrier semaphores. Data moves between devices by JAX's collectives and lax.ppermute only.
A program may use at most 64 MiB of HBM per device.

```python
import math
import jax
import jax.numpy as jnp
from jax import lax

B = 16
R = 4096
TAPS = 4
HALF = 8
LEVELS = 4
BEAMS = 256
N_SUB = 16


def with_ends(values, stream_key, least, high):
    extent = values.shape
    index_at = [jax.random.randint(jax.random.fold_in(stream_key, axis), (), 0, extent[axis]) for axis in range(len(extent))]
    values = values.at[tuple(index_at)].set(least)
    longest = extent.index(max(extent))
    index_at[longest] = (index_at[longest] + 1) % extent[longest]
    return values.at[tuple(index_at)].set(high)


def block_scale(key, extent, shards, least, high):
    def one(axis_at, parts):
        heights = jax.random.uniform(jax.random.fold_in(jax.random.fold_in(key, 6), axis_at), (parts,), jnp.float32, least / len(shards), high / len(shards))
        return jnp.repeat(jnp.exp(heights), extent[axis_at] // parts).reshape((-1,) + (1,) * (len(extent) - axis_at - 1))

    loudness = one(*shards[0])
    for cut in shards[1:]:
        loudness = loudness * one(*cut)
    return loudness


def scatter_about(own_key, dims, scale, reach, pieces=(), kind=jnp.bfloat16):
    result = jax.random.normal(own_key, dims, jnp.float32) * scale
    if len(pieces) > 0:
        result = block_scale(own_key, dims, pieces, -0.22, 0.18) * result
    return jnp.clip(result, min=-reach, max=reach).astype(kind)


def setup_inputs(seed: int = 0, part: int = 0) -> dict:
    streams_of = jax.random.split(jax.random.key(seed), 6)
    part_keys = jax.random.split(jax.random.fold_in(streams_of[5], part), 6)
    return {
        "sub_images": scatter_about(part_keys[0], (2, BEAMS, R), 1.0, 6.0, ((1, 16),), jnp.float32),
        "shift_table": with_ends(jax.random.randint(streams_of[1], (LEVELS, N_SUB, 2, HALF), -256, 257), jax.random.fold_in(streams_of[1], 1), -256, 256).astype(jnp.int32),
        "phase_table": jnp.clip(jax.random.uniform(streams_of[2], (LEVELS, N_SUB, 2, HALF), jnp.float32, -3.140625, 3.140625), -3.140625, 3.140625),
        "offset_table": with_ends(jax.random.randint(streams_of[3], (LEVELS, N_SUB, 2, B), 0, HALF - TAPS + 1), jax.random.fold_in(streams_of[3], 1), 0, HALF - TAPS).astype(jnp.int32),
        "weight_table": scatter_about(streams_of[4], (LEVELS, N_SUB, 2, TAPS, B), (2 * TAPS) ** -0.5, 2.0, ((1, 16),), jnp.float32),
    }


def signed_frequency(length):
    indices = jnp.arange(length, dtype=jnp.int32)
    return ((indices + length // 2) % length) - length // 2


def reference(sub_images, shift_table, phase_table, offset_table, weight_table):
    current = sub_images.reshape(2, N_SUB, B, R)
    indices = jnp.arange(N_SUB, dtype=jnp.int32)
    frequency = signed_frequency(R)
    columns = jnp.arange(HALF, dtype=jnp.int32)
    for level_idx in range(LEVELS):
        partner = indices ^ (1 << level_idx)
        side_bit = (indices >> level_idx) & 1
        halves = current.reshape(2, N_SUB, 2, HALF, R)
        kept_half = halves[:, indices, side_bit]
        arrived = halves[:, partner, side_bit]
        children = jnp.stack([kept_half, arrived], axis=2)
        complex_in = children[0] + 1j * children[1]
        spectrum = jnp.fft.fft(complex_in, axis=-1)
        shifts = shift_table[level_idx]
        turns = ((frequency[None, None, None, :] * shifts[..., None]) % (4 * R)).astype(phase_table.dtype)
        angles = phase_table[level_idx][..., None] - turns * (2.0 * math.pi / (4 * R))
        spectrum = spectrum * (jnp.cos(angles) + 1j * jnp.sin(angles))
        moved = jnp.fft.ifft(spectrum, axis=-1)
        offsets = offset_table[level_idx]
        weights = weight_table[level_idx]
        stencil = jnp.zeros((N_SUB, 2, B, HALF), weight_table.dtype)
        for tap_idx in range(TAPS):
            hits = (columns[None, None, None, :] == offsets[..., None] + tap_idx).astype(weight_table.dtype)
            stencil = stencil + weights[:, :, tap_idx, :, None] * hits
        real_part = jnp.einsum("icjm,icmr->ijr", stencil, jnp.real(moved), precision=lax.Precision.HIGHEST)
        imag_part = jnp.einsum("icjm,icmr->ijr", stencil, jnp.imag(moved), precision=lax.Precision.HIGHEST)
        current = jnp.stack([real_part, imag_part])
    return jnp.transpose(current.reshape(2, N_SUB * B, R), (0, 2, 1))
```

```python
import functools
import math

import jax
import jax.numpy as jnp
import numpy as np
from jax import lax
from jax.experimental import pallas as pl
from jax.experimental.pallas import tpu as pltpu
from jax.sharding import PartitionSpec as P

LANES = 128
MXU = 256
f32 = jnp.float32
bf16 = jnp.bfloat16


def swapped(block, axis, stride):
    count = lax.axis_size(axis)
    route = []
    for low in range(count):
        high = low | 1 << stride
        if high != low and high < count:
            route += [(low, high), (high, low)]
    return lax.ppermute(block, axis, route)


def whole_spec():
    return pl.BlockSpec(memory_space=pltpu.VMEM)


def call(kernel, outs, ins, scalars, scratch, flops, name):
    moved = sum(math.prod(o.shape) * o.dtype.itemsize for o in outs)
    moved += sum(math.prod(i.shape) * i.dtype.itemsize for i in ins)
    return pl.pallas_call(
        kernel,
        out_shape=outs,
        in_specs=[pl.BlockSpec(memory_space=pltpu.SMEM)] + [whole_spec()] * len(ins),
        out_specs=[whole_spec()] * len(outs),
        scratch_shapes=scratch,
        cost_estimate=pl.CostEstimate(flops=flops, bytes_accessed=moved, transcendentals=0),
        name=name,
    )(scalars, *ins)


def lane_matrix(direction, scale):
    k = np.arange(LANES)
    angle = direction * 2.0 * np.pi * (np.outer(k, k) % LANES) / LANES
    c, s = np.cos(angle) * scale, np.sin(angle) * scale
    full = np.block([[c, s], [-s, c]]).astype(np.float32)
    high = full.astype(bf16)
    low = (full - high.astype(np.float32)).astype(bf16)
    return high, low


def lane_twiddle(outer, direction):
    total = outer * LANES
    turns = np.outer(np.arange(outer), np.arange(LANES)) % total
    angle = direction * 2.0 * np.pi * turns / total
    return np.stack([np.cos(angle), np.sin(angle)]).astype(np.float32)


def times_constant(value, turn):
    real, imag = value
    turn = turn % 1.0
    if turn == 0.0:
        return value
    if turn == 0.5:
        return (-real, -imag)
    if turn == 0.25:
        return (-imag, real)
    if turn == 0.75:
        return (imag, -real)
    c, s = math.cos(2 * math.pi * turn), math.sin(2 * math.pi * turn)
    if abs(abs(c) - abs(s)) < 1e-12:
        r = abs(c)
        sc, ss = math.copysign(1, c), math.copysign(1, s)
        a = (real if sc > 0 else -real) - (imag if ss > 0 else -imag)
        b = (real if ss > 0 else -real) + (imag if sc > 0 else -imag)
        return (a * r, b * r)
    return (real * c - imag * s, real * s + imag * c)


def small_dft(values, direction):
    count = len(values)
    if count == 1:
        return values
    even = small_dft(values[0::2], direction)
    odd = small_dft(values[1::2], direction)
    first, second = [], []
    for k in range(count // 2):
        o = times_constant(odd[k], direction * k / count)
        e = even[k]
        first.append((e[0] + o[0], e[1] + o[1]))
        second.append((e[0] - o[0], e[1] - o[1]))
    return first + second


def split_factors(count):
    inner = 1 << ((count.bit_length() - 1) + 1) // 2
    return count // inner, inner


def staged_dft(count, direction, load, store, scratch):
    outer, inner = split_factors(count)
    for b in range(inner):
        got = small_dft([load(inner * a + b) for a in range(outer)], direction)
        for c in range(outer):
            value = times_constant(got[c], direction * b * c / count)
            scratch[0, c * inner + b] = value[0]
            scratch[1, c * inner + b] = value[1]
    for c in range(outer):
        line = [(scratch[0, c * inner + b], scratch[1, c * inner + b]) for b in range(inner)]
        got = small_dft(line, direction)
        for d in range(inner):
            store(c + outer * d, got[d])


def put_split(high_ref, low_ref, row, rows, value):
    for part in range(2):
        high = value[part].astype(bf16)
        low = (value[part] - high.astype(f32)).astype(bf16)
        high_ref[row : row + rows, part * LANES : (part + 1) * LANES] = high
        low_ref[row : row + rows, part * LANES : (part + 1) * LANES] = low


def dot3(left_high, left_low, right_high, right_low):
    def one(a, b):
        return jnp.dot(a, b, preferred_element_type=f32)

    return one(left_high, right_high) + (one(left_low, right_high) + one(left_high, right_low))


def put_halves(keep_ref, send_ref, bit, k, block, half):
    low, high = block[:half], block[half:]
    keep = jnp.where(bit == 0, low, high)
    send = jnp.where(bit == 0, high, low)
    for part in range(2):
        cut = slice(part * LANES, (part + 1) * LANES)
        keep_ref[part, k] = keep[:, cut]
        send_ref[part, k] = send[:, cut]


def forward_kernel(dims, bits, image, high_m, low_m, twiddle, keep, send, mid, high, low):
    rows, outer, group = dims
    half = rows // 2

    def load(q):
        cut = slice(q * LANES, (q + 1) * LANES)
        return image[0, :, cut], image[1, :, cut]

    def store(k, value):
        c, s = twiddle[0, k : k + 1, :], twiddle[1, k : k + 1, :]
        value = (value[0] * c - value[1] * s, value[0] * s + value[1] * c)
        put_split(high, low, k * rows, rows, value)

    staged_dft(outer, -1, load, store, mid)
    bit = bits[0]
    size = group * rows
    for g in range(outer // group):
        cut = slice(g * size, (g + 1) * size)
        out = dot3(high[cut], low[cut], high_m[...], low_m[...])
        for i in range(group):
            put_halves(keep, send, bit, g * group + i, out[i * rows : (i + 1) * rows], half)


def rotated(value, near, far, k):
    shape = value[0].shape
    fr = jnp.broadcast_to(far[0, :, k : k + 1], shape)
    fi = jnp.broadcast_to(far[1, :, k : k + 1], shape)
    nr, ni = near[0], near[1]
    rr, ri = nr * fr - ni * fi, nr * fi + ni * fr
    return value[0] * rr - value[1] * ri, value[0] * ri + value[1] * rr


def blended(dims, keep, arrived, near, far, blend_high, blend_low, high, low):
    rows, outer, group = dims
    size = group * rows
    for g in range(outer // group):
        for i in range(group):
            k = g * group + i
            value = tuple(
                jnp.concatenate([keep[part, k], arrived[part, k]], axis=0) for part in range(2)
            )
            put_split(high, low, k * rows, rows, rotated(value, near, far, k))
        cut = slice(g * size, (g + 1) * size)
        yield g, dot3(blend_high[...], blend_low[...], high[cut], low[cut])


def level_kernel(dims, level, bits, kept, arrived, near, far, blend_high, blend_low, keep, send, high, low):
    rows, outer, group = dims
    bit = bits[level + 1]
    for g, out in blended(dims, kept, arrived, near, far, blend_high, blend_low, high, low):
        for i in range(group):
            put_halves(keep, send, bit, g * group + i, out[i * rows : (i + 1) * rows], rows // 2)


def inverse_kernel(
    dims, per_block, bits, kept, arrived, near, far, blend_high, blend_low,
    last_near, last_far, high_m, low_m, twiddle, out_ref, mid, back, high, low,
):
    rows, outer, group = dims
    size = group * rows
    for g, out in blended(dims, kept, arrived, near, far, blend_high, blend_low, high, low):
        for i in range(group):
            k = g * group + i
            block = out[i * rows : (i + 1) * rows]
            value = rotated((block[:, :LANES], block[:, LANES:]), last_near, last_far, k)
            put_split(high, low, k * rows, rows, value)
        cut = slice(g * size, (g + 1) * size)
        out = dot3(high[cut], low[cut], high_m[...], low_m[...])
        for i in range(group):
            k = g * group + i
            block = out[i * rows : (i + 1) * rows]
            real, imag = block[:, :LANES], block[:, LANES:]
            c, s = twiddle[0, k : k + 1, :], twiddle[1, k : k + 1, :]
            back[0, k] = real * c - imag * s
            back[1, k] = real * s + imag * c

    def load(k):
        return back[0, k], back[1, k]

    def store(q, value):
        for part in range(2):
            out_ref[q // per_block, part, q % per_block] = value[part]

    staged_dft(outer, 1, load, store, mid)


def turn_kernel(dims, bits, children, blend_high, blend_low, out_ref):
    sub_count, per_block, rows = dims
    beams = sub_count * rows
    for part in range(2):
        for cut in range(per_block):
            line = children[:, part, cut].reshape(beams, LANES).T
            high = line.astype(bf16)
            low = (line - high.astype(f32)).astype(bf16)
            out_ref[part, cut * LANES : (cut + 1) * LANES, :] = dot3(
                high, low, blend_high[...], blend_low[...]
            )


def rotation_tables(shifts, phases, outer):
    full = 4 * outer * LANES
    lane = jnp.arange(LANES, dtype=jnp.int32)
    lane = outer * jnp.where(lane >= LANES // 2, lane - LANES, lane)
    turns = (shifts[..., None] * lane) % full
    angles = phases[..., None] - turns.astype(f32) * (2.0 * math.pi / full)
    near = jnp.stack([jnp.cos(angles), jnp.sin(angles)])
    step = jnp.arange(outer, dtype=jnp.int32)
    angles = ((shifts[..., None] * step) % full).astype(f32) * (2.0 * math.pi / full)
    far = jnp.stack([jnp.cos(angles), -jnp.sin(angles)])
    return near, far


def stencil_of(offsets, weights, half_beams):
    columns = jnp.arange(half_beams, dtype=jnp.int32)
    total = 0.0
    for tap in range(weights.shape[-2]):
        hits = columns == offsets[..., None] + tap
        total = total + jnp.where(hits, weights[..., tap, :, None], 0.0)
    return total


def split(table):
    high = lax.reduce_precision(table, 8, 7)
    return high.astype(bf16), (table - high).astype(bf16)


def body(sub_images, shift_table, phase_table, offset_table, weight_table):
    _, rows, range_bins = sub_images.shape
    half = rows // 2
    outer = range_bins // LANES
    group = max(1, min(outer, MXU // rows))
    sub_count = lax.axis_size("sub")
    levels = sub_count.bit_length() - 1
    last = levels - 1
    me = lax.axis_index("sub")
    taps = weight_table.shape[3]
    dims = (rows, outer, group)
    shifts = shift_table[:, 0]
    phases = phase_table[:, 0]
    offsets = offset_table[:, 0]
    weights = weight_table[:, 0]
    bits = jnp.stack([me >> level & 1 for level in range(levels)]).astype(jnp.int32)

    mine = jnp.concatenate(
        [
            shifts[last].astype(f32).reshape(-1),
            phases[last].reshape(-1),
            offsets[last].astype(f32).reshape(-1),
            weights[last].reshape(-1),
        ]
    )
    width = -(-mine.size // LANES) * LANES
    known = jnp.pad(mine, (0, width - mine.size)).reshape(-1, LANES)
    order = [last] + list(range(last))
    for at in order:
        other = swapped(known, "sub", at)
        if at == last:
            partner = other.reshape(-1)
        mine_first = (me >> at & 1) == 0
        known = jnp.stack([jnp.where(mine_first, known, other), jnp.where(mine_first, other, known)])
    axes = [len(order) - 1 - order.index(at) for at in reversed(range(levels))]
    tables = known.transpose(axes + [levels, levels + 1]).reshape(sub_count, width)
    at = 4 * half
    last_offsets = tables[:, at : at + 2 * rows].astype(jnp.int32).reshape(sub_count, 2, rows)
    at += 2 * rows
    last_weights = tables[:, at : at + 2 * taps * rows].reshape(sub_count, 2, taps, rows)
    last_stencil = stencil_of(last_offsets, last_weights, half)

    partner_shift = partner[half : 2 * half].astype(jnp.int32)
    partner_phase = partner[3 * half : 4 * half]
    own_first = bits[last] == 0
    last_shift = jnp.concatenate(
        [
            jnp.where(own_first, shifts[last, 0], partner_shift),
            jnp.where(own_first, partner_shift, shifts[last, 0]),
        ]
    )
    last_phase = jnp.concatenate(
        [
            jnp.where(own_first, phases[last, 0], partner_phase),
            jnp.where(own_first, partner_phase, phases[last, 0]),
        ]
    )
    near, far = rotation_tables(shifts[:last].reshape(last, rows), phases[:last].reshape(last, rows), outer)
    last_near, last_far = rotation_tables(last_shift, last_phase, outer)

    stencil = stencil_of(offsets[:last], weights[:last], half)
    matrix = jnp.moveaxis(stencil, 1, 2).reshape(last, rows, rows)
    eye = jnp.eye(group, dtype=f32)
    wide = eye[None, :, None, :, None] * matrix[:, None, :, None, :]
    wide_high, wide_low = split(wide.reshape(last, group * rows, group * rows))

    slab = jax.ShapeDtypeStruct((2, outer, half, LANES), f32)
    mid = pltpu.VMEM((2, outer, rows, LANES), f32)
    halves = [pltpu.VMEM((outer * rows, 2 * LANES), bf16)] * 2
    flops = 3 * 2 * outer * rows * MXU * MXU

    keep, send = call(
        functools.partial(forward_kernel, dims),
        [slab, slab],
        [sub_images, *lane_matrix(-1, 1.0), lane_twiddle(outer, -1)],
        bits,
        [mid] + halves,
        flops,
        "forward",
    )
    for level in range(last - 1):
        arrived = swapped(send, "sub", level)
        keep, send = call(
            functools.partial(level_kernel, dims, level),
            [slab, slab],
            [keep, arrived, near[:, level], far[:, level], wide_high[level], wide_low[level]],
            bits,
            halves,
            flops,
            "level",
        )
    level = last - 1
    arrived = swapped(send, "sub", level)
    block = range_bins // sub_count
    direct = block % LANES == 0
    per_block = block // LANES if direct else 1
    (children,) = call(
        functools.partial(inverse_kernel, dims, per_block),
        [jax.ShapeDtypeStruct((outer // per_block, 2, per_block, rows, LANES), f32)],
        [
            keep, arrived, near[:, level], far[:, level], wide_high[level], wide_low[level],
            last_near, last_far, *lane_matrix(1, 1.0 / range_bins), lane_twiddle(outer, 1),
        ],
        bits,
        [mid, mid] + halves,
        2 * flops,
        "inverse",
    )
    index = jnp.arange(sub_count, dtype=jnp.int32)
    if direct and sub_count * rows <= MXU:
        gathered = lax.all_to_all(
            children.reshape(sub_count, 2 * per_block * rows, LANES), "sub", 0, 0, tiled=True
        ).reshape(sub_count, 2, per_block, rows, LANES)
        side = index >> last & 1
        halves_of = jnp.arange(2, dtype=jnp.int32)
        source = index[:, None, None]
        target = index[None, None, :]
        right_half = halves_of[None, :, None] == side[None, None, :]
        own = (source == target) & right_half
        crossed = (source == (target ^ (1 << last))) & right_half
        first = last_stencil[:, 0].transpose(2, 0, 1)
        second = last_stencil[:, 1].transpose(2, 0, 1)
        blend = jnp.where(own[:, :, None, :, None], first[None, None], 0.0)
        blend = blend + jnp.where(crossed[:, :, None, :, None], second[None, None], 0.0)
        blend_high, blend_low = split(blend.reshape(sub_count * rows, sub_count * rows))
        (turned,) = call(
            functools.partial(turn_kernel, (sub_count, per_block, rows)),
            [jax.ShapeDtypeStruct((2, block, sub_count * rows), f32)],
            [gathered, blend_high, blend_low],
            bits,
            [],
            flops,
            "turn",
        )
        return turned
    line = children.reshape(sub_count, outer // sub_count, 2, rows, LANES) if direct else (
        children.reshape(outer, 2, rows, LANES // block, block).transpose(0, 3, 1, 2, 4)
    )
    if direct:
        line = line.transpose(0, 2, 3, 1, 4)
    line = line.reshape(sub_count, 2 * rows, block)
    gathered = lax.all_to_all(line, "sub", 0, 0, tiled=True)
    gathered = gathered.reshape(sub_count, 2, 2, half, block)
    side = (index >> last & 1)[:, None, None, None]
    chosen = jnp.where(side == 0, gathered[:, :, 0], gathered[:, :, 1])
    crossing = gathered[index ^ (1 << last)]
    crossing = jnp.where(side == 0, crossing[:, :, 0], crossing[:, :, 1])
    both = jnp.concatenate([chosen, crossing], axis=2)
    matrix = jnp.moveaxis(last_stencil, 1, 2).reshape(sub_count, rows, rows)
    merged = jnp.einsum("ijm,ipmq->pqij", matrix, both, precision=lax.Precision.HIGHEST)
    return merged.reshape(2, block, sub_count * rows)


def solution(mesh):
    placed = (
        P(None, ("img", "sub"), None),
        P(None, "sub", None, None),
        P(None, "sub", None, None),
        P(None, "sub", None, None),
        P(None, "sub", None, None, None),
    )
    return jax.shard_map(
        body, mesh=mesh, in_specs=placed, out_specs=P(None, ("img", "sub"), None), check_vma=False
    )
```

```python
import functools
import math

import jax
import jax.numpy as jnp
import numpy as np
from jax import lax
from jax.experimental import pallas as pl
from jax.experimental.pallas import tpu as pltpu
from jax.sharding import PartitionSpec as P

LANES = 128
MXU = 256
VMEM_GRANT = 12 << 20
f32 = jnp.float32
bf16 = jnp.bfloat16


def swapped(block, axis, stride):
    count = lax.axis_size(axis)
    route = []
    for low in range(count):
        high = low | 1 << stride
        if high != low and high < count:
            route += [(low, high), (high, low)]
    return lax.ppermute(block, axis, route)


def call(kernel, outs, ins, scratch, flops, name):
    moved = sum(math.prod(o.shape) * o.dtype.itemsize for o in outs)
    moved += sum(math.prod(i.shape) * i.dtype.itemsize for i in ins)
    return pl.pallas_call(
        kernel,
        out_shape=outs,
        in_specs=[pl.BlockSpec(memory_space=pltpu.VMEM)] * len(ins),
        out_specs=[pl.BlockSpec(memory_space=pltpu.VMEM)] * len(outs),
        scratch_shapes=scratch,
        cost_estimate=pl.CostEstimate(flops=flops, bytes_accessed=moved, transcendentals=0),
        compiler_params=pltpu.CompilerParams(vmem_limit_bytes=VMEM_GRANT),
        name=name,
    )(*ins)


def lane_matrix(direction, scale):
    k = np.arange(LANES)
    angle = direction * 2.0 * np.pi * (np.outer(k, k) % LANES) / LANES
    c, s = np.cos(angle) * scale, np.sin(angle) * scale
    full = np.block([[c, s], [-s, c]]).astype(np.float32)
    high = full.astype(bf16)
    low = (full - high.astype(np.float32)).astype(bf16)
    return high, low


def lane_twiddle(outer, direction):
    total = outer * LANES
    turns = np.outer(np.arange(outer), np.arange(LANES)) % total
    angle = direction * 2.0 * np.pi * turns / total
    return np.stack([np.cos(angle), np.sin(angle)]).astype(np.float32)


def times_constant(value, turn):
    real, imag = value
    turn = turn % 1.0
    if turn == 0.0:
        return value
    if turn == 0.5:
        return (-real, -imag)
    if turn == 0.25:
        return (-imag, real)
    if turn == 0.75:
        return (imag, -real)
    c, s = math.cos(2 * math.pi * turn), math.sin(2 * math.pi * turn)
    if abs(abs(c) - abs(s)) < 1e-12:
        r = abs(c)
        sc, ss = math.copysign(1, c), math.copysign(1, s)
        a = (real if sc > 0 else -real) - (imag if ss > 0 else -imag)
        b = (real if ss > 0 else -real) + (imag if sc > 0 else -imag)
        return (a * r, b * r)
    return (real * c - imag * s, real * s + imag * c)


def small_dft(values, direction):
    count = len(values)
    if count == 1:
        return values
    even = small_dft(values[0::2], direction)
    odd = small_dft(values[1::2], direction)
    first, second = [], []
    for k in range(count // 2):
        o = times_constant(odd[k], direction * k / count)
        e = even[k]
        first.append((e[0] + o[0], e[1] + o[1]))
        second.append((e[0] - o[0], e[1] - o[1]))
    return first + second


def split_factors(count):
    inner = 1 << ((count.bit_length() - 1) + 1) // 2
    return count // inner, inner


def staged_dft(count, direction, load, store, scratch):
    outer, inner = split_factors(count)
    for b in range(inner):
        got = small_dft([load(inner * a + b) for a in range(outer)], direction)
        for c in range(outer):
            value = times_constant(got[c], direction * b * c / count)
            scratch[0, c * inner + b] = value[0]
            scratch[1, c * inner + b] = value[1]
    for c in range(outer):
        line = [(scratch[0, c * inner + b], scratch[1, c * inner + b]) for b in range(inner)]
        got = small_dft(line, direction)
        for d in range(inner):
            store(c + outer * d, got[d])


def put_split(high_ref, low_ref, row, rows, value):
    for part in range(2):
        high = value[part].astype(bf16)
        low = (value[part] - high.astype(f32)).astype(bf16)
        high_ref[row : row + rows, part * LANES : (part + 1) * LANES] = high
        low_ref[row : row + rows, part * LANES : (part + 1) * LANES] = low


def dot3(left_high, left_low, right_high, right_low):
    def one(a, b):
        return jnp.dot(a, b, preferred_element_type=f32)

    return one(left_high, right_high) + (one(left_low, right_high) + one(left_high, right_low))


def put_halves(keep_ref, send_ref, bit, outer, k, block, half):
    low, high = block[:half], block[half:]
    keep = jnp.where(bit == 0, low, high)
    send = jnp.where(bit == 0, high, low)
    for part in range(2):
        cut = slice(part * LANES, (part + 1) * LANES)
        keep_ref[part * outer + k] = keep[:, cut]
        send_ref[part * outer + k] = send[:, cut]


def cos_sin(turns, full):
    quarter = full // 4
    turns = turns & (full - 1)
    quadrant = (turns + quarter // 2) >> (quarter.bit_length() - 1)
    x = (turns - quadrant * quarter).astype(f32) * (2.0 * math.pi / full)
    y = x * x
    sine, cosine = 0.0, 0.0
    for term in (9, 7, 5, 3, 1):
        sine = sine * y + (-1.0) ** (term // 2) / math.factorial(term)
    for term in (10, 8, 6, 4, 2, 0):
        cosine = cosine * y + (-1.0) ** (term // 2) / math.factorial(term)
    sine = sine * x
    odd = (quadrant & 1) == 1
    first = jnp.where(odd, sine, cosine)
    second = jnp.where(odd, cosine, sine)
    first = jnp.where(((quadrant + 1) & 2) == 2, -first, first)
    return first, jnp.where((quadrant & 2) == 2, -second, second)


class Sizes:
    def __init__(self, rows, outer, taps, sub_count):
        self.rows, self.outer, self.taps, self.sub_count = rows, outer, taps, sub_count
        self.half = rows // 2
        self.levels = sub_count.bit_length() - 1
        self.last = self.levels - 1
        self.group = max(1, min(outer, MXU // rows))
        self.at_offset = 2 * taps
        self.at_shift = self.at_offset + 2
        self.at_phase = self.at_shift + 2
        self.record = -(-(self.at_phase + 2) // 8) * 8
        self.pages = -(-self.levels * self.record // LANES)
        self.slots = LANES // rows
        self.blocks = -(-sub_count // self.slots)
        self.known = self.blocks * self.record // 8
        self.last_page = self.last * self.record // LANES


def prep_kernel(z, shift, phase, offset, weight, tabs, pack, lines):
    me = lax.axis_index("sub")
    lines[...] = jnp.zeros_like(lines)
    for level in range(z.levels):
        at = level * z.record
        for c in range(2):
            lines[at + c * z.taps : at + (c + 1) * z.taps, : z.rows] = weight[level, 0, c]
        at += z.at_offset
        lines[at : at + 2, : z.rows] = offset[level, 0].astype(f32)
        lines[at + 2 : at + 4, : z.half] = shift[level, 0].astype(f32)
        lines[at + 4 : at + 6, : z.half] = phase[level, 0]
    for page in range(z.pages):
        turned = lines[page * LANES : (page + 1) * LANES, :].T[: z.rows]
        tabs[:, page * LANES : (page + 1) * LANES] = turned
        if page == z.last_page:
            pack[: z.rows] = turned
    spread = lines[z.last * z.record : (z.last + 1) * z.record, :]
    step = z.rows
    while step < LANES:
        spread = spread + pltpu.roll(spread, step, 1)
        step *= 2
    slot = lax.broadcasted_iota(jnp.int32, spread.shape, 1) // z.rows
    for block in range(z.blocks):
        at = z.rows + block * z.record
        pack[at : at + z.record] = jnp.where(slot + block * z.slots == me, spread, 0.0)


def tables_kernel(z, tabs, pack, other, near, far, wide_high, wide_low):
    me = lax.axis_index("sub")
    full = 4 * z.outer * LANES
    shape = (z.rows, LANES)
    lane = lax.broadcasted_iota(jnp.int32, shape, 1)
    signed = z.outer * jnp.where(lane >= LANES // 2, lane - LANES, lane)

    def children(table, at):
        return [table[: z.half, at + c : at + c + 1] for c in range(2)]

    for level in range(z.levels):
        at = level * z.record
        shifts, phases = children(tabs, at + z.at_shift), children(tabs, at + z.at_phase)
        if level == z.last:
            away = at - z.last_page * LANES
            theirs = children(other, away + z.at_shift)[1], children(other, away + z.at_phase)[1]
            low = (me >> level & 1) == 0
            for mine, their in zip((shifts, phases), theirs):
                first = mine[0]
                mine[0] = jnp.where(low, first, their)
                mine[1] = jnp.where(low, their, first)
        shifts = jnp.broadcast_to(jnp.concatenate(shifts, axis=0), shape).astype(jnp.int32)
        phases = jnp.broadcast_to(jnp.concatenate(phases, axis=0), shape)
        c, s = cos_sin(shifts * signed, full)
        pc, ps = jnp.cos(phases), jnp.sin(phases)
        near[level, 0] = pc * c + ps * s
        near[level, 1] = ps * c - pc * s
        c, s = cos_sin(shifts * lane, full)
        far[level, 0] = c
        far[level, 1] = -s

    size = z.group * z.rows
    shape = (z.rows, size)
    column = lax.broadcasted_iota(jnp.int32, shape, 1)
    beam = column % z.half
    child = (column // z.half) % 2
    block = column // z.rows
    for level in range(z.last):
        at = level * z.record
        wide = jnp.zeros(shape, f32)
        for c in range(2):
            first = tabs[:, at + z.at_offset + c : at + z.at_offset + c + 1].astype(jnp.int32)
            for tap in range(z.taps):
                hits = (beam == first + tap) & (child == c)
                wide += jnp.where(hits, tabs[:, at + c * z.taps + tap : at + c * z.taps + tap + 1], 0.0)
        for i in range(z.group):
            value = jnp.where(block == i, wide, 0.0)
            high = value.astype(bf16)
            wide_high[level, i * z.rows : (i + 1) * z.rows] = high
            wide_low[level, i * z.rows : (i + 1) * z.rows] = (value - high.astype(f32)).astype(bf16)


def last_blend_kernel(z, known, blend_high, blend_low):
    beams = z.sub_count * z.rows
    for block in range(beams // LANES):
        table = known[block * z.record : (block + 1) * z.record]
        shape = (z.rows, LANES)
        row = lax.broadcasted_iota(jnp.int32, shape, 0)
        owner = lax.broadcasted_iota(jnp.int32, shape, 1) // z.rows + block * z.slots
        mine = (row // z.half) == (owner >> z.last & 1)
        parts = []
        for c in range(2):
            first = jnp.broadcast_to(table[z.at_offset + c : z.at_offset + c + 1].astype(jnp.int32), shape)
            total = jnp.zeros(shape, f32)
            for tap in range(z.taps):
                hits = (row % z.half == first + tap) & mine
                line = jnp.broadcast_to(table[c * z.taps + tap : c * z.taps + tap + 1], shape)
                total += jnp.where(hits, line, 0.0)
            parts.append(total)
        for source in range(z.sub_count):
            value = jnp.where(owner == source, parts[0], 0.0)
            value = jnp.where(owner == source ^ (1 << z.last), parts[1], value)
            high = value.astype(bf16)
            at = (slice(source * z.rows, (source + 1) * z.rows), slice(block * LANES, (block + 1) * LANES))
            blend_high[at] = high
            blend_low[at] = (value - high.astype(f32)).astype(bf16)


def forward_kernel(z, image, high_m, low_m, twiddle, keep, send, mid, high, low):
    def load(q):
        cut = slice(q * LANES, (q + 1) * LANES)
        return image[0, :, cut], image[1, :, cut]

    def store(k, value):
        c, s = twiddle[0, k : k + 1, :], twiddle[1, k : k + 1, :]
        value = (value[0] * c - value[1] * s, value[0] * s + value[1] * c)
        put_split(high, low, k * z.rows, z.rows, value)

    staged_dft(z.outer, -1, load, store, mid)
    bit = lax.axis_index("sub") & 1
    size = z.group * z.rows
    for g in range(z.outer // z.group):
        cut = slice(g * size, (g + 1) * size)
        out = dot3(high[cut], low[cut], high_m[...], low_m[...])
        for i in range(z.group):
            block = out[i * z.rows : (i + 1) * z.rows]
            put_halves(keep, send, bit, z.outer, g * z.group + i, block, z.half)


def rotated(value, near, far, k):
    shape = value[0].shape
    fr = jnp.broadcast_to(far[0][:, k : k + 1], shape)
    fi = jnp.broadcast_to(far[1][:, k : k + 1], shape)
    nr, ni = near[0], near[1]
    rr, ri = nr * fr - ni * fi, nr * fi + ni * fr
    return value[0] * rr - value[1] * ri, value[0] * ri + value[1] * rr


def blended(z, level, keep, arrived, near, far, wide_high, wide_low, high, low):
    size = z.group * z.rows
    close = near[level, 0], near[level, 1]
    steps = far[level, 0], far[level, 1]
    for g in range(z.outer // z.group):
        for i in range(z.group):
            k = g * z.group + i
            value = tuple(
                jnp.concatenate([keep[part * z.outer + k], arrived[part * z.outer + k]], axis=0)
                for part in range(2)
            )
            put_split(high, low, k * z.rows, z.rows, rotated(value, close, steps, k))
        cut = slice(g * size, (g + 1) * size)
        yield g, dot3(wide_high[level], wide_low[level], high[cut], low[cut])


def level_kernel(z, level, kept, arrived, held, near, far, wide_high, wide_low, keep, send, high, low):
    slabs = 2 * z.outer
    bit = lax.axis_index("sub") >> (level + 1) & 1
    if level == 0:
        send[slabs:] = held[...]
    else:
        send[slabs:] = held[slabs:] + arrived[slabs:]
    for g, out in blended(z, level, kept, arrived, near, far, wide_high, wide_low, high, low):
        for i in range(z.group):
            block = out[i * z.rows : (i + 1) * z.rows]
            put_halves(keep, send, bit, z.outer, g * z.group + i, block, z.half)


def inverse_kernel(
    z, per_block, kept, arrived, held, near, far, wide_high, wide_low, high_m, low_m, twiddle,
    out_ref, known, mid, back, high, low,
):
    slabs = 2 * z.outer
    size = z.group * z.rows
    level = z.last - 1
    known[...] = held[slabs:] + arrived[slabs:] if level > 0 else held[...]
    close = near[z.last, 0], near[z.last, 1]
    steps = far[z.last, 0], far[z.last, 1]
    for g, out in blended(z, level, kept, arrived, near, far, wide_high, wide_low, high, low):
        for i in range(z.group):
            k = g * z.group + i
            block = out[i * z.rows : (i + 1) * z.rows]
            value = rotated((block[:, :LANES], block[:, LANES:]), close, steps, k)
            put_split(high, low, k * z.rows, z.rows, value)
        cut = slice(g * size, (g + 1) * size)
        out = dot3(high[cut], low[cut], high_m[...], low_m[...])
        for i in range(z.group):
            k = g * z.group + i
            block = out[i * z.rows : (i + 1) * z.rows]
            real, imag = block[:, :LANES], block[:, LANES:]
            c, s = twiddle[0, k : k + 1, :], twiddle[1, k : k + 1, :]
            back[0, k] = real * c - imag * s
            back[1, k] = real * s + imag * c

    def load(k):
        return back[0, k], back[1, k]

    def store(q, value):
        for part in range(2):
            out_ref[q // per_block, part, q % per_block] = value[part]

    staged_dft(z.outer, 1, load, store, mid)


def turn_kernel(z, per_block, children, blend_high, blend_low, out_ref):
    beams = z.sub_count * z.rows
    for part in range(2):
        for cut in range(per_block):
            line = children[:, part, cut].reshape(beams, LANES).T
            high = line.astype(bf16)
            low = (line - high.astype(f32)).astype(bf16)
            out_ref[part, cut * LANES : (cut + 1) * LANES, :] = dot3(
                high, low, blend_high[...], blend_low[...]
            )


def body(sub_images, shift_table, phase_table, offset_table, weight_table):
    _, rows, range_bins = sub_images.shape
    outer = range_bins // LANES
    sub_count = lax.axis_size("sub")
    z = Sizes(rows, outer, weight_table.shape[3], sub_count)
    size = z.group * rows
    flops = 3 * 2 * outer * rows * MXU * MXU
    shape = jax.ShapeDtypeStruct

    tabs, pack = call(
        functools.partial(prep_kernel, z),
        [shape((rows, z.pages * LANES), f32), shape((rows + z.blocks * z.record, LANES), f32)],
        [shift_table, phase_table, offset_table, weight_table],
        [pltpu.VMEM((z.pages * LANES, LANES), f32)],
        1 << 16,
        "prep",
    )
    other = swapped(pack, "sub", z.last)

    slabs = 2 * outer
    slab = shape((slabs, z.half, LANES), f32)
    longer = shape((slabs + z.known, z.half, LANES), f32)
    mid = pltpu.VMEM((2, outer, rows, LANES), f32)
    halves = [pltpu.VMEM((outer * rows, 2 * LANES), bf16)] * 2

    keep, send = call(
        functools.partial(forward_kernel, z),
        [slab, slab],
        [sub_images, *lane_matrix(-1, 1.0), lane_twiddle(outer, -1)],
        [mid] + halves,
        flops,
        "forward",
    )
    held = pack[rows:] + other[rows:]
    arrived = swapped(send, "sub", 0)
    held = (held + swapped(held, "sub", 0)).reshape(z.known, 8, LANES)
    tables = call(
        functools.partial(tables_kernel, z),
        [shape((z.levels, 2, rows, LANES), f32)] * 2 + [shape((z.last, size, size), bf16)] * 2,
        [tabs, pack, other],
        [],
        1 << 20,
        "tables",
    )
    for level in range(z.last - 1):
        keep, send = call(
            functools.partial(level_kernel, z, level),
            [slab, longer],
            [keep, arrived, held, *tables],
            halves,
            flops,
            "level",
        )
        held = send
        arrived = swapped(send, "sub", level + 1)
    block = range_bins // sub_count
    direct = block % LANES == 0
    per_block = block // LANES if direct else 1
    children, known = call(
        functools.partial(inverse_kernel, z, per_block),
        [
            shape((outer // per_block, 2, per_block, rows, LANES), f32),
            shape((z.known, 8, LANES), f32),
        ],
        [keep, arrived, held, *tables, *lane_matrix(1, 1.0 / range_bins), lane_twiddle(outer, 1)],
        [mid, mid] + halves,
        2 * flops,
        "inverse",
    )
    known = known.reshape(z.blocks * z.record, LANES)
    beams = sub_count * rows
    if direct and beams <= MXU:
        gathered = lax.all_to_all(
            children.reshape(sub_count, 2 * per_block * rows, LANES), "sub", 0, 0, tiled=True
        ).reshape(sub_count, 2, per_block, rows, LANES)
        blend = call(
            functools.partial(last_blend_kernel, z),
            [shape((beams, beams), bf16)] * 2,
            [known],
            [],
            1 << 18,
            "blend",
        )
        (turned,) = call(
            functools.partial(turn_kernel, z, per_block),
            [shape((2, block, beams), f32)],
            [gathered, *blend],
            [],
            flops,
            "turn",
        )
        return turned
    return wide_turn(z, block, direct, children, known)


def wide_turn(z, block, direct, children, known):
    sub_count, rows, half = z.sub_count, z.rows, z.half
    if direct:
        line = children.transpose(0, 1, 3, 2, 4)
    else:
        line = children.reshape(z.outer, 2, rows, LANES // block, block).transpose(0, 3, 1, 2, 4)
    gathered = lax.all_to_all(line.reshape(sub_count, 2 * rows, block), "sub", 0, 0, tiled=True)
    gathered = gathered.reshape(sub_count, 2, 2, half, block)
    table = known.reshape(z.blocks, z.record, z.slots, rows).transpose(0, 2, 1, 3)
    table = table.reshape(-1, z.record, rows)[:sub_count]
    weights = table[:, : z.at_offset].reshape(sub_count, 2, z.taps, rows)
    offsets = table[:, z.at_offset : z.at_shift].astype(jnp.int32)
    columns = jnp.arange(half, dtype=jnp.int32)
    stencil = 0.0
    for tap in range(z.taps):
        hits = columns == offsets[..., None] + tap
        stencil = stencil + jnp.where(hits, weights[:, :, tap, :, None], 0.0)
    index = jnp.arange(sub_count, dtype=jnp.int32)
    side = (index >> z.last & 1)[:, None, None, None]
    chosen = jnp.where(side == 0, gathered[:, :, 0], gathered[:, :, 1])
    crossing = gathered[index ^ (1 << z.last)]
    crossing = jnp.where(side == 0, crossing[:, :, 0], crossing[:, :, 1])
    both = jnp.concatenate([chosen, crossing], axis=2)
    matrix = jnp.moveaxis(stencil, 1, 2).reshape(sub_count, rows, rows)
    merged = jnp.einsum("ijm,ipmq->pqij", matrix, both, precision=lax.Precision.HIGHEST)
    return merged.reshape(2, block, sub_count * rows)


def solution(mesh):
    placed = (
        P(None, ("img", "sub"), None),
        P(None, "sub", None, None),
        P(None, "sub", None, None),
        P(None, "sub", None, None),
        P(None, "sub", None, None, None),
    )
    return jax.shard_map(
        body, mesh=mesh, in_specs=placed, out_specs=P(None, ("img", "sub"), None), check_vma=False
    )
```

```python
import functools
import math

import jax
import jax.numpy as jnp
import numpy as np
from jax import lax
from jax.experimental import pallas as pl
from jax.experimental.pallas import tpu as pltpu
from jax.sharding import PartitionSpec as P

LANES = 128
MXU = 256
VMEM_GRANT = 12 << 20
f32 = jnp.float32
bf16 = jnp.bfloat16


def swapped(block, axis, stride):
    count = lax.axis_size(axis)
    route = []
    for low in range(count):
        high = low | 1 << stride
        if high != low and high < count:
            route += [(low, high), (high, low)]
    return lax.ppermute(block, axis, route)


def call(kernel, outs, ins, scratch, flops, name, after=(), space=pltpu.VMEM):
    moved = sum(math.prod(o.shape) * o.dtype.itemsize for o in outs)
    moved += sum(math.prod(i.shape) * i.dtype.itemsize for i in ins)
    count = len(ins)

    def run(*refs):
        kernel(*refs[:count], *refs[count + len(after) :])

    return pl.pallas_call(
        run,
        out_shape=outs,
        in_specs=[pl.BlockSpec(memory_space=space)] * count
        + [pl.BlockSpec(memory_space=pl.ANY)] * len(after),
        out_specs=[pl.BlockSpec(memory_space=pltpu.VMEM)] * len(outs),
        scratch_shapes=scratch,
        cost_estimate=pl.CostEstimate(flops=flops, bytes_accessed=moved, transcendentals=0),
        compiler_params=pltpu.CompilerParams(vmem_limit_bytes=VMEM_GRANT),
        name=name,
    )(*ins, *after)


def lane_matrix(direction, scale):
    k = np.arange(LANES)
    angle = direction * 2.0 * np.pi * (np.outer(k, k) % LANES) / LANES
    c, s = np.cos(angle) * scale, np.sin(angle) * scale
    full = np.block([[c, s], [-s, c]]).astype(np.float32)
    high = full.astype(bf16)
    low = (full - high.astype(np.float32)).astype(bf16)
    return high, low


def lane_twiddle(outer, direction):
    total = outer * LANES
    turns = np.outer(np.arange(outer), np.arange(LANES)) % total
    angle = direction * 2.0 * np.pi * turns / total
    return np.stack([np.cos(angle), np.sin(angle)]).astype(np.float32)


def times_constant(value, turn):
    real, imag = value
    turn = turn % 1.0
    if turn == 0.0:
        return value
    if turn == 0.5:
        return (-real, -imag)
    if turn == 0.25:
        return (-imag, real)
    if turn == 0.75:
        return (imag, -real)
    c, s = math.cos(2 * math.pi * turn), math.sin(2 * math.pi * turn)
    if abs(abs(c) - abs(s)) < 1e-12:
        r = abs(c)
        sc, ss = math.copysign(1, c), math.copysign(1, s)
        a = (real if sc > 0 else -real) - (imag if ss > 0 else -imag)
        b = (real if ss > 0 else -real) + (imag if sc > 0 else -imag)
        return (a * r, b * r)
    return (real * c - imag * s, real * s + imag * c)


def small_dft(values, direction):
    count = len(values)
    if count == 1:
        return values
    even = small_dft(values[0::2], direction)
    odd = small_dft(values[1::2], direction)
    first, second = [], []
    for k in range(count // 2):
        o = times_constant(odd[k], direction * k / count)
        e = even[k]
        first.append((e[0] + o[0], e[1] + o[1]))
        second.append((e[0] - o[0], e[1] - o[1]))
    return first + second


def split_factors(count):
    inner = 1 << ((count.bit_length() - 1) + 1) // 2
    return count // inner, inner


def staged_dft(count, direction, load, store, scratch):
    outer, inner = split_factors(count)
    for b in range(inner):
        got = small_dft([load(inner * a + b) for a in range(outer)], direction)
        for c in range(outer):
            value = times_constant(got[c], direction * b * c / count)
            scratch[0, c * inner + b] = value[0]
            scratch[1, c * inner + b] = value[1]
    for c in range(outer):
        line = [(scratch[0, c * inner + b], scratch[1, c * inner + b]) for b in range(inner)]
        got = small_dft(line, direction)
        for d in range(inner):
            store(c + outer * d, got[d])


def put_split(high_ref, low_ref, row, rows, value):
    for part in range(2):
        high = value[part].astype(bf16)
        low = (value[part] - high.astype(f32)).astype(bf16)
        high_ref[row : row + rows, part * LANES : (part + 1) * LANES] = high
        low_ref[row : row + rows, part * LANES : (part + 1) * LANES] = low


def dot3(left_high, left_low, right_high, right_low):
    def one(a, b):
        return jnp.dot(a, b, preferred_element_type=f32)

    return one(left_high, right_high) + (one(left_low, right_high) + one(left_high, right_low))


def put_halves(keep_ref, send_ref, bit, group, i, block, half):
    low, high = block[:half], block[half:]
    keep = jnp.where(bit == 0, low, high)
    send = jnp.where(bit == 0, high, low)
    for part in range(2):
        cut = slice(part * LANES, (part + 1) * LANES)
        keep_ref[part * group + i] = keep[:, cut]
        send_ref[part * group + i] = send[:, cut]


def cos_sin(turns, full):
    quarter = full // 4
    turns = turns & (full - 1)
    quadrant = (turns + quarter // 2) >> (quarter.bit_length() - 1)
    x = (turns - quadrant * quarter).astype(f32) * (2.0 * math.pi / full)
    y = x * x
    sine, cosine = 0.0, 0.0
    for term in (9, 7, 5, 3, 1):
        sine = sine * y + (-1.0) ** (term // 2) / math.factorial(term)
    for term in (10, 8, 6, 4, 2, 0):
        cosine = cosine * y + (-1.0) ** (term // 2) / math.factorial(term)
    sine = sine * x
    odd = (quadrant & 1) == 1
    first = jnp.where(odd, sine, cosine)
    second = jnp.where(odd, cosine, sine)
    first = jnp.where(((quadrant + 1) & 2) == 2, -first, first)
    return first, jnp.where((quadrant & 2) == 2, -second, second)


class Sizes:
    def __init__(self, rows, outer, taps, sub_count):
        self.rows, self.outer, self.taps, self.sub_count = rows, outer, taps, sub_count
        self.half = rows // 2
        self.levels = sub_count.bit_length() - 1
        self.last = self.levels - 1
        self.group = max(1, min(outer, MXU // rows))
        self.at_offset = 2 * taps
        self.at_shift = self.at_offset + 2
        self.at_phase = self.at_shift + 2
        self.record = -(-(self.at_phase + 2) // 8) * 8
        self.pages = -(-self.levels * self.record // LANES)
        self.slots = LANES // rows
        self.blocks = -(-sub_count // self.slots)
        self.chunks = outer // self.group
        self.last_page = self.last * self.record // LANES


def prepare(z, shift, phase, offset, weight, tabs, pack, lines):
    me = lax.axis_index("sub")
    lines[...] = jnp.zeros_like(lines)
    for level in range(z.levels):
        at = level * z.record
        for c in range(2):
            lines[at + c * z.taps : at + (c + 1) * z.taps, : z.rows] = weight[level, 0, c]
        at += z.at_offset
        lines[at : at + 2, : z.rows] = offset[level, 0].astype(f32)
        lines[at + 2 : at + 4, : z.half] = shift[level, 0].astype(f32)
        lines[at + 4 : at + 6, : z.half] = phase[level, 0]
    for page in range(z.pages):
        turned = lines[page * LANES : (page + 1) * LANES, :].T[: z.rows]
        tabs[:, page * LANES : (page + 1) * LANES] = turned
        if page == z.last_page:
            pack[: z.rows] = turned
    spread = lines[z.last * z.record : (z.last + 1) * z.record, :]
    step = z.rows
    while step < LANES:
        spread = spread + pltpu.roll(spread, step, 1)
        step *= 2
    slot = lax.broadcasted_iota(jnp.int32, spread.shape, 1) // z.rows
    for block in range(z.blocks):
        at = z.rows + block * z.record
        pack[at : at + z.record] = jnp.where(slot + block * z.slots == me, spread, 0.0)


def rotation(z, shifts, phases, near, far):
    full = 4 * z.outer * LANES
    shape = (z.rows, LANES)
    lane = lax.broadcasted_iota(jnp.int32, shape, 1)
    signed = z.outer * jnp.where(lane >= LANES // 2, lane - LANES, lane)
    shifts = jnp.broadcast_to(jnp.concatenate(shifts, axis=0), shape).astype(jnp.int32)
    phases = jnp.broadcast_to(jnp.concatenate(phases, axis=0), shape)
    c, s = cos_sin(shifts * signed, full)
    pc, ps = jnp.cos(phases), jnp.sin(phases)
    near[0] = pc * c + ps * s
    near[1] = ps * c - pc * s
    c, s = cos_sin(shifts * lane, full)
    far[0] = c
    far[1] = -s


def of_children(z, table, at):
    return [table[: z.half, at + c : at + c + 1] for c in range(2)]


def last_tables_kernel(z, pack, other, near, far):
    low = (lax.axis_index("sub") >> z.last & 1) == 0
    at = z.last * z.record - z.last_page * LANES
    both = []
    for row in (z.at_shift, z.at_phase):
        mine = of_children(z, pack, at + row)[0]
        their = of_children(z, other, at + row)[1]
        both.append([jnp.where(low, mine, their), jnp.where(low, their, mine)])
    rotation(z, *both, near, far)


def tables_kernel(z, tabs, near, far, wide_high, wide_low):
    for level in range(z.last):
        at = level * z.record
        shifts, phases = of_children(z, tabs, at + z.at_shift), of_children(z, tabs, at + z.at_phase)
        rotation(z, shifts, phases, near.at[level], far.at[level])
    size = z.group * z.rows
    shape = (z.rows, size)
    column = lax.broadcasted_iota(jnp.int32, shape, 1)
    beam = column % z.half
    child = (column // z.half) % 2
    block = column // z.rows
    for level in range(z.last):
        at = level * z.record
        wide = jnp.zeros(shape, f32)
        for c in range(2):
            first = tabs[:, at + z.at_offset + c : at + z.at_offset + c + 1].astype(jnp.int32)
            for tap in range(z.taps):
                hits = (beam == first + tap) & (child == c)
                wide += jnp.where(hits, tabs[:, at + c * z.taps + tap : at + c * z.taps + tap + 1], 0.0)
        for i in range(z.group):
            value = jnp.where(block == i, wide, 0.0)
            high = value.astype(bf16)
            wide_high[level, i * z.rows : (i + 1) * z.rows] = high
            wide_low[level, i * z.rows : (i + 1) * z.rows] = (value - high.astype(f32)).astype(bf16)


def last_blend_kernel(z, known, blend_high, blend_low):
    me = lax.axis_index("sub")
    beams = z.sub_count * z.rows
    for block in range(beams // LANES):
        table = known[block * z.record : (block + 1) * z.record]
        shape = (z.rows, LANES)
        row = lax.broadcasted_iota(jnp.int32, shape, 0)
        owner = lax.broadcasted_iota(jnp.int32, shape, 1) // z.rows + block * z.slots
        mine = (row // z.half) == (owner >> z.last & 1)
        parts = []
        for c in range(2):
            first = jnp.broadcast_to(table[z.at_offset + c : z.at_offset + c + 1].astype(jnp.int32), shape)
            total = jnp.zeros(shape, f32)
            for tap in range(z.taps):
                hits = (row % z.half == first + tap) & mine
                line = jnp.broadcast_to(table[c * z.taps + tap : c * z.taps + tap + 1], shape)
                total += jnp.where(hits, line, 0.0)
            parts.append(total)
        for away in range(z.sub_count):
            source = me ^ away
            value = jnp.where(owner == source, parts[0], 0.0)
            value = jnp.where(owner == (source ^ (1 << z.last)), parts[1], value)
            high = value.astype(bf16)
            at = (slice(away * z.rows, (away + 1) * z.rows), slice(block * LANES, (block + 1) * LANES))
            blend_high[at] = high
            blend_low[at] = (value - high.astype(f32)).astype(bf16)


def start_kernel(z, *refs):
    sources, refs = refs[:8], refs[8:]
    tabs, pack, refs = refs[0], refs[1], refs[2:]
    keeps, sends, refs = refs[: z.chunks], refs[z.chunks : 2 * z.chunks], refs[2 * z.chunks :]
    held, (lines, mid, high, low, sems) = refs[:8], refs[8:]
    copies = [
        pltpu.make_async_copy(source, place, sems.at[i])
        for i, (source, place) in enumerate(zip(sources, held))
    ]
    for copy in copies:
        copy.start()
    for copy in copies[:4]:
        copy.wait()
    prepare(z, *held[:4], tabs, pack, lines)
    image, twiddle, high_m, low_m = held[4:]
    copies[4].wait()
    copies[5].wait()

    def load(q):
        cut = slice(q * LANES, (q + 1) * LANES)
        return image[0, :, cut], image[1, :, cut]

    def store(k, value):
        c, s = twiddle[0, k : k + 1, :], twiddle[1, k : k + 1, :]
        value = (value[0] * c - value[1] * s, value[0] * s + value[1] * c)
        put_split(high, low, k * z.rows, z.rows, value)

    staged_dft(z.outer, -1, load, store, mid)
    bit = lax.axis_index("sub") & 1
    size = z.group * z.rows
    copies[6].wait()
    copies[7].wait()
    for g in range(z.chunks):
        cut = slice(g * size, (g + 1) * size)
        out = dot3(high[cut], low[cut], high_m[...], low_m[...])
        for i in range(z.group):
            block = out[i * z.rows : (i + 1) * z.rows]
            put_halves(keeps[g], sends[g], bit, z.group, i, block, z.half)


def rotated(value, near, far, k):
    shape = value[0].shape
    fr = jnp.broadcast_to(far[0][:, k : k + 1], shape)
    fi = jnp.broadcast_to(far[1][:, k : k + 1], shape)
    nr, ni = near[0], near[1]
    rr, ri = nr * fr - ni * fi, nr * fi + ni * fr
    return value[0] * rr - value[1] * ri, value[0] * ri + value[1] * rr


def blended(z, level, chunk, keep, arrived, near, far, wide_high, wide_low, high, low):
    close = near[level, 0], near[level, 1]
    steps = far[level, 0], far[level, 1]
    for i in range(z.group):
        value = tuple(
            jnp.concatenate([keep[part * z.group + i], arrived[part * z.group + i]], axis=0)
            for part in range(2)
        )
        value = rotated(value, close, steps, chunk * z.group + i)
        put_split(high, low, i * z.rows, z.rows, value)
    return dot3(wide_high[level], wide_low[level], high[...], low[...])


def level_kernel(z, level, chunk, kept, arrived, near, far, wide_high, wide_low, keep, send, high, low):
    bit = lax.axis_index("sub") >> (level + 1) & 1
    out = blended(z, level, chunk, kept, arrived, near, far, wide_high, wide_low, high, low)
    for i in range(z.group):
        put_halves(keep, send, bit, z.group, i, out[i * z.rows : (i + 1) * z.rows], z.half)


def return_kernel(
    z, chunk, kept, arrived, near, far, wide_high, wide_low, last_near, last_far,
    high_m, low_m, twiddle, back, high, low,
):
    out = blended(z, z.last - 1, chunk, kept, arrived, near, far, wide_high, wide_low, high, low)
    close = last_near[0], last_near[1]
    steps = last_far[0], last_far[1]
    for i in range(z.group):
        block = out[i * z.rows : (i + 1) * z.rows]
        value = rotated((block[:, :LANES], block[:, LANES:]), close, steps, chunk * z.group + i)
        put_split(high, low, i * z.rows, z.rows, value)
    out = dot3(high[...], low[...], high_m[...], low_m[...])
    for i in range(z.group):
        k = chunk * z.group + i
        block = out[i * z.rows : (i + 1) * z.rows]
        real, imag = block[:, :LANES], block[:, LANES:]
        c, s = twiddle[0, k : k + 1, :], twiddle[1, k : k + 1, :]
        back[0, i] = real * c - imag * s
        back[1, i] = real * s + imag * c


def gather_back(z, backs, store, mid):
    def load(k):
        back, i = backs[k // z.group], k % z.group
        return back[0, i], back[1, i]

    staged_dft(z.outer, 1, load, store, mid)


def ranges_kernel(z, *refs):
    backs, out_ref, mid = refs[: z.chunks], refs[z.chunks], refs[z.chunks + 1]

    def store(q, value):
        for part in range(2):
            out_ref[q, part] = value[part]

    gather_back(z, backs, store, mid)


def deal_kernel(z, per_block, *refs):
    pairs = z.sub_count // 2
    backs, outs = refs[: z.chunks], refs[z.chunks : z.chunks + pairs]
    mid, whole = refs[z.chunks + pairs :]

    def store(q, value):
        for part in range(2):
            at = (part * per_block + q % per_block) * z.rows
            whole[q // per_block, at : at + z.rows] = value[part]

    gather_back(z, backs, store, mid)
    me = lax.axis_index("sub")
    for k in range(pairs):
        for side in range(2):
            outs[k][side] = whole[me ^ (2 * k + side)]


def stack_kernel(*refs):
    for i, ref in enumerate(refs[:-1]):
        refs[-1][i] = ref[1]


def turn_kernel(z, per_block, *refs):
    pairs = z.sub_count // 2
    direct, passed = refs[:pairs], refs[pairs : pairs + 2]
    blend_high, blend_low, out_ref = refs[pairs + 2 :]
    for part in range(2):
        for cut in range(per_block):
            at = (part * per_block + cut) * z.rows
            at = slice(at, at + z.rows)
            line = []
            for k in range(pairs):
                line += [direct[k][0, at], passed[2 * k // pairs][k % (pairs // 2), at]]
            line = jnp.concatenate(line, axis=0).T
            high = line.astype(bf16)
            low = (line - high.astype(f32)).astype(bf16)
            out_ref[part, cut * LANES : (cut + 1) * LANES, :] = dot3(
                high, low, blend_high[...], blend_low[...]
            )


def body(sub_images, shift_table, phase_table, offset_table, weight_table):
    _, rows, range_bins = sub_images.shape
    outer = range_bins // LANES
    sub_count = lax.axis_size("sub")
    z = Sizes(rows, outer, weight_table.shape[3], sub_count)
    size = z.group * rows
    flops = 3 * 2 * size * MXU * MXU
    shape = jax.ShapeDtypeStruct
    mid = pltpu.VMEM((2, outer, rows, LANES), f32)
    halves = [pltpu.VMEM((size, 2 * LANES), bf16)] * 2
    slab = shape((2 * z.group, z.half, LANES), f32)

    sources = [shift_table, phase_table, offset_table, weight_table, sub_images]
    sources += [jnp.asarray(table) for table in (lane_twiddle(outer, -1), *lane_matrix(-1, 1.0))]
    sources = [pltpu.with_memory_space_constraint(source, pltpu.HBM) for source in sources]
    tabs, pack, *parts = call(
        functools.partial(start_kernel, z),
        [shape((rows, z.pages * LANES), f32), shape((rows + z.blocks * z.record, LANES), f32)]
        + [slab] * (2 * z.chunks),
        sources,
        [pltpu.VMEM(source.shape, source.dtype) for source in sources]
        + [pltpu.VMEM((z.pages * LANES, LANES), f32), mid]
        + [pltpu.VMEM((outer * rows, 2 * LANES), bf16)] * 2
        + [pltpu.SemaphoreType.DMA((len(sources),))],
        flops * z.chunks,
        "start",
        space=pltpu.HBM,
    )
    keeps, sends = parts[: z.chunks], parts[z.chunks :]
    arrived = [swapped(send, "sub", 0) for send in sends]
    tables = call(
        functools.partial(tables_kernel, z),
        [shape((z.last, 2, rows, LANES), f32)] * 2 + [shape((z.last, size, size), bf16)] * 2,
        [tabs],
        [],
        1 << 20,
        "tables",
    )
    other = swapped(pack, "sub", z.last)
    known = pack[rows:] + other[rows:]
    for level in range(z.last - 1):
        for chunk in range(z.chunks):
            keeps[chunk], sends[chunk] = call(
                functools.partial(level_kernel, z, level, chunk),
                [slab, slab],
                [keeps[chunk], arrived[chunk], *tables],
                halves,
                flops,
                "level",
                after=(known,) if level > 0 and chunk == 0 else (),
            )
            arrived[chunk] = swapped(sends[chunk], "sub", level + 1)
        known = known + swapped(known, "sub", level)
    last_tables = call(
        functools.partial(last_tables_kernel, z),
        [shape((2, rows, LANES), f32)] * 2,
        [pack, other],
        [],
        1 << 16,
        "last_tables",
    )
    way_back = [*lane_matrix(1, 1.0 / range_bins), lane_twiddle(outer, 1)]
    backs = [
        call(
            functools.partial(return_kernel, z, chunk),
            [shape((2, z.group, rows, LANES), f32)],
            [keeps[chunk], arrived[chunk], *tables, *last_tables, *way_back],
            halves,
            2 * flops,
            "return",
            after=(known,) if chunk == 0 else (),
        )[0]
        for chunk in range(z.chunks)
    ]
    known = known + swapped(known, "sub", z.last - 1)
    block = range_bins // sub_count
    beams = sub_count * rows
    if block % LANES or beams > MXU or sub_count < 4:
        (children,) = call(
            functools.partial(ranges_kernel, z),
            [shape((outer, 2, rows, LANES), f32)],
            backs,
            [mid],
            flops,
            "ranges",
        )
        return wide_turn(z, block, children, known)
    per_block = block // LANES
    pairs = sub_count // 2
    lines = 2 * per_block * rows
    dealt = call(
        functools.partial(deal_kernel, z, per_block),
        [shape((2, lines, LANES), f32)] * pairs,
        backs,
        [mid, pltpu.VMEM((sub_count, lines, LANES), f32)],
        flops,
        "deal",
        after=(known,),
    )
    direct = [dealt[0]]
    for k in range(1, pairs):
        route = [(i, i ^ (2 * k)) for i in range(sub_count)]
        direct.append(lax.ppermute(dealt[k], "sub", route))
    passed = []
    for start in (0, pairs // 2):
        stop = start + pairs // 2
        (both,) = call(
            stack_kernel,
            [shape((pairs // 2, lines, LANES), f32)],
            direct[start:stop],
            [],
            1,
            "stack",
        )
        passed.append(swapped(both, "sub", 0))
    blend = call(
        functools.partial(last_blend_kernel, z),
        [shape((beams, beams), bf16)] * 2,
        [known],
        [],
        1 << 18,
        "blend",
    )
    (turned,) = call(
        functools.partial(turn_kernel, z, per_block),
        [shape((2, block, beams), f32)],
        [*direct, *passed, *blend],
        [],
        flops,
        "turn",
    )
    return turned


def wide_turn(z, block, children, known):
    sub_count, rows, half = z.sub_count, z.rows, z.half
    if block % LANES == 0:
        line = children.reshape(sub_count, block // LANES, 2, rows, LANES).transpose(0, 2, 3, 1, 4)
    else:
        line = children.reshape(z.outer, 2, rows, LANES // block, block).transpose(0, 3, 1, 2, 4)
    gathered = lax.all_to_all(line.reshape(sub_count, 2 * rows, block), "sub", 0, 0, tiled=True)
    gathered = gathered.reshape(sub_count, 2, 2, half, block)
    table = known.reshape(z.blocks, z.record, z.slots, rows).transpose(0, 2, 1, 3)
    table = table.reshape(-1, z.record, rows)[:sub_count]
    weights = table[:, : z.at_offset].reshape(sub_count, 2, z.taps, rows)
    offsets = table[:, z.at_offset : z.at_shift].astype(jnp.int32)
    columns = jnp.arange(half, dtype=jnp.int32)
    stencil = 0.0
    for tap in range(z.taps):
        hits = columns == offsets[..., None] + tap
        stencil = stencil + jnp.where(hits, weights[:, :, tap, :, None], 0.0)
    index = jnp.arange(sub_count, dtype=jnp.int32)
    side = (index >> z.last & 1)[:, None, None, None]
    chosen = jnp.where(side == 0, gathered[:, :, 0], gathered[:, :, 1])
    crossing = gathered[index ^ (1 << z.last)]
    crossing = jnp.where(side == 0, crossing[:, :, 0], crossing[:, :, 1])
    both = jnp.concatenate([chosen, crossing], axis=2)
    matrix = jnp.moveaxis(stencil, 1, 2).reshape(sub_count, rows, rows)
    merged = jnp.einsum("ijm,ipmq->pqij", matrix, both, precision=lax.Precision.HIGHEST)
    return merged.reshape(2, block, sub_count * rows)


def solution(mesh):
    placed = (
        P(None, ("img", "sub"), None),
        P(None, "sub", None, None),
        P(None, "sub", None, None),
        P(None, "sub", None, None),
        P(None, "sub", None, None, None),
    )
    return jax.shard_map(
        body, mesh=mesh, in_specs=placed, out_specs=P(None, ("img", "sub"), None), check_vma=False
    )
```

```python
import functools
import math

import jax
import jax.numpy as jnp
import numpy as np
from jax import lax
from jax.experimental import pallas as pl
from jax.experimental.pallas import tpu as pltpu
from jax.sharding import PartitionSpec as P

LANES = 128
MXU = 256
VMEM_GRANT = 12 << 20
f32 = jnp.float32
bf16 = jnp.bfloat16


def swapped(block, axis, stride):
    count = lax.axis_size(axis)
    route = []
    for low in range(count):
        high = low | 1 << stride
        if high != low and high < count:
            route += [(low, high), (high, low)]
    return lax.ppermute(block, axis, route)


def call(kernel, outs, ins, scratch, flops, name, after=(), space=pltpu.VMEM):
    moved = sum(math.prod(o.shape) * o.dtype.itemsize for o in outs)
    moved += sum(math.prod(i.shape) * i.dtype.itemsize for i in ins)
    count = len(ins)

    def run(*refs):
        kernel(*refs[:count], *refs[count + len(after) :])

    return pl.pallas_call(
        run,
        out_shape=outs,
        in_specs=[pl.BlockSpec(memory_space=space)] * count
        + [pl.BlockSpec(memory_space=pl.ANY)] * len(after),
        out_specs=[pl.BlockSpec(memory_space=pltpu.VMEM)] * len(outs),
        scratch_shapes=scratch,
        cost_estimate=pl.CostEstimate(flops=flops, bytes_accessed=moved, transcendentals=0),
        compiler_params=pltpu.CompilerParams(vmem_limit_bytes=VMEM_GRANT),
        name=name,
    )(*ins, *after)


def lane_matrix(direction, scale):
    k = np.arange(LANES)
    angle = direction * 2.0 * np.pi * (np.outer(k, k) % LANES) / LANES
    c, s = np.cos(angle) * scale, np.sin(angle) * scale
    full = np.block([[c, s], [-s, c]]).astype(np.float32)
    high = full.astype(bf16)
    low = (full - high.astype(np.float32)).astype(bf16)
    return high, low


def lane_twiddle(outer, direction):
    total = outer * LANES
    turns = np.outer(np.arange(outer), np.arange(LANES)) % total
    angle = direction * 2.0 * np.pi * turns / total
    return np.stack([np.cos(angle), np.sin(angle)]).astype(np.float32)


def times_constant(value, turn):
    real, imag = value
    turn = turn % 1.0
    if turn == 0.0:
        return value
    if turn == 0.5:
        return (-real, -imag)
    if turn == 0.25:
        return (-imag, real)
    if turn == 0.75:
        return (imag, -real)
    c, s = math.cos(2 * math.pi * turn), math.sin(2 * math.pi * turn)
    if abs(abs(c) - abs(s)) < 1e-12:
        r = abs(c)
        sc, ss = math.copysign(1, c), math.copysign(1, s)
        a = (real if sc > 0 else -real) - (imag if ss > 0 else -imag)
        b = (real if ss > 0 else -real) + (imag if sc > 0 else -imag)
        return (a * r, b * r)
    return (real * c - imag * s, real * s + imag * c)


def small_dft(values, direction):
    count = len(values)
    if count == 1:
        return values
    even = small_dft(values[0::2], direction)
    odd = small_dft(values[1::2], direction)
    first, second = [], []
    for k in range(count // 2):
        o = times_constant(odd[k], direction * k / count)
        e = even[k]
        first.append((e[0] + o[0], e[1] + o[1]))
        second.append((e[0] - o[0], e[1] - o[1]))
    return first + second


def split_factors(count):
    inner = 1 << ((count.bit_length() - 1) + 1) // 2
    return count // inner, inner


def staged_dft(count, direction, load, store, scratch):
    outer, inner = split_factors(count)
    for b in range(inner):
        got = small_dft([load(inner * a + b) for a in range(outer)], direction)
        for c in range(outer):
            value = times_constant(got[c], direction * b * c / count)
            scratch[0, c * inner + b] = value[0]
            scratch[1, c * inner + b] = value[1]
    for c in range(outer):
        line = [(scratch[0, c * inner + b], scratch[1, c * inner + b]) for b in range(inner)]
        got = small_dft(line, direction)
        for d in range(inner):
            store(c + outer * d, got[d])


def put_split(high_ref, low_ref, row, rows, value):
    for part in range(2):
        high = value[part].astype(bf16)
        low = (value[part] - high.astype(f32)).astype(bf16)
        high_ref[row : row + rows, part * LANES : (part + 1) * LANES] = high
        low_ref[row : row + rows, part * LANES : (part + 1) * LANES] = low


def dot3(left_high, left_low, right_high, right_low):
    def one(a, b):
        return jnp.dot(a, b, preferred_element_type=f32)

    return one(left_high, right_high) + (one(left_low, right_high) + one(left_high, right_low))


def put_halves(keep_ref, send_ref, bit, group, i, block, half):
    low, high = block[:half], block[half:]
    keep = jnp.where(bit == 0, low, high)
    send = jnp.where(bit == 0, high, low)
    for part in range(2):
        cut = slice(part * LANES, (part + 1) * LANES)
        keep_ref[part * group + i] = keep[:, cut]
        send_ref[part * group + i] = send[:, cut]


def cos_sin(turns, full):
    quarter = full // 4
    turns = turns & (full - 1)
    quadrant = (turns + quarter // 2) >> (quarter.bit_length() - 1)
    x = (turns - quadrant * quarter).astype(f32) * (2.0 * math.pi / full)
    y = x * x
    sine, cosine = 0.0, 0.0
    for term in (9, 7, 5, 3, 1):
        sine = sine * y + (-1.0) ** (term // 2) / math.factorial(term)
    for term in (10, 8, 6, 4, 2, 0):
        cosine = cosine * y + (-1.0) ** (term // 2) / math.factorial(term)
    sine = sine * x
    odd = (quadrant & 1) == 1
    first = jnp.where(odd, sine, cosine)
    second = jnp.where(odd, cosine, sine)
    first = jnp.where(((quadrant + 1) & 2) == 2, -first, first)
    return first, jnp.where((quadrant & 2) == 2, -second, second)


class Sizes:
    def __init__(self, rows, outer, taps, sub_count):
        self.rows, self.outer, self.taps, self.sub_count = rows, outer, taps, sub_count
        self.half = rows // 2
        self.levels = sub_count.bit_length() - 1
        self.last = self.levels - 1
        self.group = max(1, min(outer, MXU // rows))
        self.at_offset = 2 * taps
        self.at_shift = self.at_offset + 2
        self.at_phase = self.at_shift + 2
        self.record = -(-(self.at_phase + 2) // 8) * 8
        self.pages = -(-self.levels * self.record // LANES)
        self.slots = LANES // rows
        self.blocks = -(-sub_count // self.slots)
        self.chunks = outer // self.group
        self.last_page = self.last * self.record // LANES


def prepare(z, shift, phase, offset, weight, tabs, pack, lines):
    me = lax.axis_index("sub")
    lines[...] = jnp.zeros_like(lines)
    for level in range(z.levels):
        at = level * z.record
        for c in range(2):
            lines[at + c * z.taps : at + (c + 1) * z.taps, : z.rows] = weight[level, 0, c]
        at += z.at_offset
        lines[at : at + 2, : z.rows] = offset[level, 0].astype(f32)
        lines[at + 2 : at + 4, : z.half] = shift[level, 0].astype(f32)
        lines[at + 4 : at + 6, : z.half] = phase[level, 0]
    for page in range(z.pages):
        turned = lines[page * LANES : (page + 1) * LANES, :].T[: z.rows]
        tabs[:, page * LANES : (page + 1) * LANES] = turned
        if page == z.last_page:
            pack[: z.rows] = turned
    spread = lines[z.last * z.record : (z.last + 1) * z.record, :]
    step = z.rows
    while step < LANES:
        spread = spread + pltpu.roll(spread, step, 1)
        step *= 2
    slot = lax.broadcasted_iota(jnp.int32, spread.shape, 1) // z.rows
    for block in range(z.blocks):
        at = z.rows + block * z.record
        pack[at : at + z.record] = jnp.where(slot + block * z.slots == me, spread, 0.0)


def rotation(z, shifts, phases, near, far):
    full = 4 * z.outer * LANES
    shape = (z.rows, LANES)
    lane = lax.broadcasted_iota(jnp.int32, shape, 1)
    signed = z.outer * jnp.where(lane >= LANES // 2, lane - LANES, lane)
    shifts = jnp.broadcast_to(jnp.concatenate(shifts, axis=0), shape).astype(jnp.int32)
    phases = jnp.broadcast_to(jnp.concatenate(phases, axis=0), shape)
    c, s = cos_sin(shifts * signed, full)
    pc, ps = jnp.cos(phases), jnp.sin(phases)
    near[0] = pc * c + ps * s
    near[1] = ps * c - pc * s
    c, s = cos_sin(shifts * lane, full)
    far[0] = c
    far[1] = -s


def of_children(z, table, at):
    return [table[: z.half, at + c : at + c + 1] for c in range(2)]


def last_tables_kernel(z, pack, other, near, far):
    low = (lax.axis_index("sub") >> z.last & 1) == 0
    at = z.last * z.record - z.last_page * LANES
    both = []
    for row in (z.at_shift, z.at_phase):
        mine = of_children(z, pack, at + row)[0]
        their = of_children(z, other, at + row)[1]
        both.append([jnp.where(low, mine, their), jnp.where(low, their, mine)])
    rotation(z, *both, near, far)


def tables_kernel(z, tabs, near, far, wide_high, wide_low):
    for level in range(z.last):
        at = level * z.record
        shifts, phases = of_children(z, tabs, at + z.at_shift), of_children(z, tabs, at + z.at_phase)
        rotation(z, shifts, phases, near.at[level], far.at[level])
    size = z.group * z.rows
    shape = (z.rows, size)
    column = lax.broadcasted_iota(jnp.int32, shape, 1)
    beam = column % z.half
    child = (column // z.half) % 2
    block = column // z.rows
    for level in range(z.last):
        at = level * z.record
        wide = jnp.zeros(shape, f32)
        for c in range(2):
            first = tabs[:, at + z.at_offset + c : at + z.at_offset + c + 1].astype(jnp.int32)
            for tap in range(z.taps):
                hits = (beam == first + tap) & (child == c)
                wide += jnp.where(hits, tabs[:, at + c * z.taps + tap : at + c * z.taps + tap + 1], 0.0)
        for i in range(z.group):
            value = jnp.where(block == i, wide, 0.0)
            high = value.astype(bf16)
            wide_high[level, i * z.rows : (i + 1) * z.rows] = high
            wide_low[level, i * z.rows : (i + 1) * z.rows] = (value - high.astype(f32)).astype(bf16)


def last_blend_kernel(z, masks, skips, *refs):
    blend_high, blend_low = refs[-2:]
    known = refs[0][...]
    for ref, skip in zip(refs[1:-2], skips):
        known = known + ref[skip:]
    me = lax.axis_index("sub")
    beams = z.sub_count * z.rows
    for block in range(beams // LANES):
        table = known[block * z.record : (block + 1) * z.record]
        shape = (z.rows, LANES)
        row = lax.broadcasted_iota(jnp.int32, shape, 0)
        owner = lax.broadcasted_iota(jnp.int32, shape, 1) // z.rows + block * z.slots
        mine = (row // z.half) == (owner >> z.last & 1)
        parts = []
        for c in range(2):
            first = jnp.broadcast_to(table[z.at_offset + c : z.at_offset + c + 1].astype(jnp.int32), shape)
            total = jnp.zeros(shape, f32)
            for tap in range(z.taps):
                hits = (row % z.half == first + tap) & mine
                line = jnp.broadcast_to(table[c * z.taps + tap : c * z.taps + tap + 1], shape)
                total += jnp.where(hits, line, 0.0)
            parts.append(total)
        for e in range(z.sub_count):
            source = me ^ span(masks, e)
            value = jnp.where(owner == source, parts[0], 0.0)
            value = jnp.where(owner == (source ^ (1 << z.last)), parts[1], value)
            high = value.astype(bf16)
            at = (slice(e * z.rows, (e + 1) * z.rows), slice(block * LANES, (block + 1) * LANES))
            blend_high[at] = high
            blend_low[at] = (value - high.astype(f32)).astype(bf16)


def start_kernel(z, *refs):
    sources, refs = refs[:8], refs[8:]
    tabs, pack, refs = refs[0], refs[1], refs[2:]
    keeps, sends, refs = refs[: z.chunks], refs[z.chunks : 2 * z.chunks], refs[2 * z.chunks :]
    held, (lines, mid, high, low, sems) = refs[:8], refs[8:]
    copies = [
        pltpu.make_async_copy(source, place, sems.at[i])
        for i, (source, place) in enumerate(zip(sources, held))
    ]
    for copy in copies:
        copy.start()
    for copy in copies[:4]:
        copy.wait()
    prepare(z, *held[:4], tabs, pack, lines)
    image, twiddle, high_m, low_m = held[4:]
    copies[4].wait()
    copies[5].wait()

    def load(q):
        cut = slice(q * LANES, (q + 1) * LANES)
        return image[0, :, cut], image[1, :, cut]

    def store(k, value):
        c, s = twiddle[0, k : k + 1, :], twiddle[1, k : k + 1, :]
        value = (value[0] * c - value[1] * s, value[0] * s + value[1] * c)
        put_split(high, low, k * z.rows, z.rows, value)

    staged_dft(z.outer, -1, load, store, mid)
    bit = lax.axis_index("sub") & 1
    size = z.group * z.rows
    copies[6].wait()
    copies[7].wait()
    for g in range(z.chunks):
        cut = slice(g * size, (g + 1) * size)
        out = dot3(high[cut], low[cut], high_m[...], low_m[...])
        for i in range(z.group):
            block = out[i * z.rows : (i + 1) * z.rows]
            put_halves(keeps[g], sends[g], bit, z.group, i, block, z.half)


def rotated(value, near, far, k):
    shape = value[0].shape
    fr = jnp.broadcast_to(far[0][:, k : k + 1], shape)
    fi = jnp.broadcast_to(far[1][:, k : k + 1], shape)
    nr, ni = near[0], near[1]
    rr, ri = nr * fr - ni * fi, nr * fi + ni * fr
    return value[0] * rr - value[1] * ri, value[0] * ri + value[1] * rr


def blended(z, level, chunk, keep, arrived, near, far, wide_high, wide_low, high, low):
    close = near[level, 0], near[level, 1]
    steps = far[level, 0], far[level, 1]
    for i in range(z.group):
        value = tuple(
            jnp.concatenate([keep[part * z.group + i], arrived[part * z.group + i]], axis=0)
            for part in range(2)
        )
        value = rotated(value, close, steps, chunk * z.group + i)
        put_split(high, low, i * z.rows, z.rows, value)
    return dot3(wide_high[level], wide_low[level], high[...], low[...])


def level_kernel(z, level, chunk, kept, arrived, near, far, wide_high, wide_low, keep, send, high, low):
    bit = lax.axis_index("sub") >> (level + 1) & 1
    out = blended(z, level, chunk, kept, arrived, near, far, wide_high, wide_low, high, low)
    for i in range(z.group):
        put_halves(keep, send, bit, z.group, i, out[i * z.rows : (i + 1) * z.rows], z.half)


def return_kernel(
    z, chunk, kept, arrived, near, far, wide_high, wide_low, last_near, last_far,
    high_m, low_m, twiddle, back, high, low,
):
    out = blended(z, z.last - 1, chunk, kept, arrived, near, far, wide_high, wide_low, high, low)
    close = last_near[0], last_near[1]
    steps = last_far[0], last_far[1]
    for i in range(z.group):
        block = out[i * z.rows : (i + 1) * z.rows]
        value = rotated((block[:, :LANES], block[:, LANES:]), close, steps, chunk * z.group + i)
        put_split(high, low, i * z.rows, z.rows, value)
    out = dot3(high[...], low[...], high_m[...], low_m[...])
    for i in range(z.group):
        k = chunk * z.group + i
        block = out[i * z.rows : (i + 1) * z.rows]
        real, imag = block[:, :LANES], block[:, LANES:]
        c, s = twiddle[0, k : k + 1, :], twiddle[1, k : k + 1, :]
        back[0, i] = real * c - imag * s
        back[1, i] = real * s + imag * c


def gather_back(z, backs, store, mid):
    def load(k):
        back, i = backs[k // z.group], k % z.group
        return back[0, i], back[1, i]

    staged_dft(z.outer, 1, load, store, mid)


def ranges_kernel(z, *refs):
    backs, out_ref, mid = refs[: z.chunks], refs[z.chunks], refs[z.chunks + 1]

    def store(q, value):
        for part in range(2):
            out_ref[q, part] = value[part]

    gather_back(z, backs, store, mid)


def span(masks, e):
    away = 0
    for at, mask in enumerate(masks):
        if e >> at & 1:
            away ^= mask
    return away


def deal_kernel(z, per_block, masks, firsts, *refs):
    parts = 2 * per_block
    backs, refs = refs[: z.chunks], refs[z.chunks :]
    outs, (mid, whole) = refs[: 2 * parts], refs[2 * parts :]

    def store(q, value):
        for part in range(2):
            whole[part * per_block + q % per_block, q // per_block] = value[part]

    gather_back(z, backs, store, mid)
    me = lax.axis_index("sub")
    for part in range(parts):
        for side in range(2):
            chosen = [e for e in range(z.sub_count) if (e >> firsts[part] & 1) == side]
            for i, e in enumerate(chosen):
                at = slice(i * z.rows, (i + 1) * z.rows)
                outs[2 * part + side][at] = whole[part, me ^ span(masks, e)]


def pack_kernel(z, places, held, *refs):
    out = refs[-1]
    for i, (array, at) in enumerate(places):
        out[i * z.rows : (i + 1) * z.rows] = refs[array][at * z.rows : (at + 1) * z.rows]
    if held:
        start = len(places) * z.rows
        total = refs[len(refs) - 1 - len(held)][...]
        for ref, skip in zip(refs[len(refs) - len(held) : -1], held[1:]):
            total = total + ref[skip:]
        out[start:] = total


def turn_kernel(z, per_block, places, *refs):
    counts = [1 + max(array for array, _ in place.values()) for place in places]
    blend_high, blend_low, out_ref = refs[sum(counts) :]
    for part in range(2 * per_block):
        arrays = refs[sum(counts[:part]) : sum(counts[: part + 1])]
        line = []
        for e in range(z.sub_count):
            array, at = places[part][e]
            line.append(arrays[array][at * z.rows : (at + 1) * z.rows])
        line = jnp.concatenate(line, axis=0).T
        high = line.astype(bf16)
        low = (line - high.astype(f32)).astype(bf16)
        a, cut = part // per_block, part % per_block
        out_ref[a, cut * LANES : (cut + 1) * LANES, :] = dot3(high, low, blend_high[...], blend_low[...])


def body(sub_images, shift_table, phase_table, offset_table, weight_table):
    _, rows, range_bins = sub_images.shape
    outer = range_bins // LANES
    sub_count = lax.axis_size("sub")
    z = Sizes(rows, outer, weight_table.shape[3], sub_count)
    size = z.group * rows
    flops = 3 * 2 * size * MXU * MXU
    shape = jax.ShapeDtypeStruct
    mid = pltpu.VMEM((2, outer, rows, LANES), f32)
    halves = [pltpu.VMEM((size, 2 * LANES), bf16)] * 2
    slab = shape((2 * z.group, z.half, LANES), f32)

    sources = [shift_table, phase_table, offset_table, weight_table, sub_images]
    sources += [jnp.asarray(table) for table in (lane_twiddle(outer, -1), *lane_matrix(-1, 1.0))]
    sources = [pltpu.with_memory_space_constraint(source, pltpu.HBM) for source in sources]
    tabs, pack, *parts = call(
        functools.partial(start_kernel, z),
        [shape((rows, z.pages * LANES), f32), shape((rows + z.blocks * z.record, LANES), f32)]
        + [slab] * (2 * z.chunks),
        sources,
        [pltpu.VMEM(source.shape, source.dtype) for source in sources]
        + [pltpu.VMEM((z.pages * LANES, LANES), f32), mid]
        + [pltpu.VMEM((outer * rows, 2 * LANES), bf16)] * 2
        + [pltpu.SemaphoreType.DMA((len(sources),))],
        flops * z.chunks,
        "start",
        space=pltpu.HBM,
    )
    keeps, sends = parts[: z.chunks], parts[z.chunks :]
    arrived = [swapped(send, "sub", 0) for send in sends]
    tables = call(
        functools.partial(tables_kernel, z),
        [shape((z.last, 2, rows, LANES), f32)] * 2 + [shape((z.last, size, size), bf16)] * 2,
        [tabs],
        [],
        1 << 20,
        "tables",
    )
    other = swapped(pack, "sub", z.last)
    known = pack[rows:] + other[rows:]
    for level in range(z.last - 1):
        for chunk in range(z.chunks):
            keeps[chunk], sends[chunk] = call(
                functools.partial(level_kernel, z, level, chunk),
                [slab, slab],
                [keeps[chunk], arrived[chunk], *tables],
                halves,
                flops,
                "level",
                after=(known,) if level == 1 and chunk == 0 else (),
            )
            arrived[chunk] = swapped(sends[chunk], "sub", level + 1)
        if level == 0:
            known = known + swapped(known, "sub", 0)
    last_tables = call(
        functools.partial(last_tables_kernel, z),
        [shape((2, rows, LANES), f32)] * 2,
        [pack, other],
        [],
        1 << 16,
        "last_tables",
    )
    way_back = [*lane_matrix(1, 1.0 / range_bins), lane_twiddle(outer, 1)]
    backs = [
        call(
            functools.partial(return_kernel, z, chunk),
            [shape((2, z.group, rows, LANES), f32)],
            [keeps[chunk], arrived[chunk], *tables, *last_tables, *way_back],
            halves,
            2 * flops,
            "return",
        )[0]
        for chunk in range(z.chunks)
    ]
    block = range_bins // sub_count
    beams = sub_count * rows
    if block % LANES or beams > MXU or sub_count < 8:
        (children,) = call(
            functools.partial(ranges_kernel, z),
            [shape((outer, 2, rows, LANES), f32)],
            backs,
            [mid],
            flops,
            "ranges",
        )
        for level in range(1 if z.last > 1 else 0, z.last):
            known = known + swapped(known, "sub", level)
        return wide_turn(z, block, children, known)

    per_block = block // LANES
    parts = 2 * per_block
    masks = [1 << level for level in range(z.last)] + [3 << (z.last - 1)]
    orders = [[(part + step) % z.levels for step in range(z.levels)] for part in range(parts)]
    half_lines = sub_count // 2 * rows
    dealt = call(
        functools.partial(deal_kernel, z, per_block, masks, [order[0] for order in orders]),
        [shape((half_lines, LANES), f32)] * (2 * parts),
        backs,
        [mid, pltpu.VMEM((parts, sub_count, rows, LANES), f32)],
        flops,
        "deal",
    )

    def exchanged(array, mask):
        return lax.ppermute(array, "sub", [(i, i ^ mask) for i in range(sub_count)])

    arrays, places, ready = [], [], []
    records = [known]
    for part in range(parts):
        first = orders[part][0]
        place = {}
        for side in range(2):
            chosen = [e for e in range(sub_count) if (e >> first & 1) == side]
            place.update({e: (side, i) for i, e in enumerate(chosen)})
        arrays.append([dealt[2 * part]])
        places.append(place)
        ready.append(dealt[2 * part + 1])
    for step in range(z.levels):
        for part in range(parts):
            dim = orders[part][step]
            place, have = places[part], arrays[part]
            if step > 0:
                chosen = [e for e in range(sub_count) if e >> dim & 1]
                riding = records if part == 0 and 0 < dim < z.last else []
                skips = [0] + [half_lines] * (len(riding) - 1)
                lines = half_lines + (known.shape[0] if riding else 0)
                (ready[part],) = call(
                    functools.partial(pack_kernel, z, [place[e] for e in chosen], skips if riding else []),
                    [shape((lines, LANES), f32)],
                    [*have, *riding],
                    [],
                    1,
                    "pack",
                )
                places[part] = place = {**place, **{e: (len(have), i) for i, e in enumerate(chosen)}}
                if riding:
                    records.append(None)
            got = exchanged(ready[part], masks[dim])
            have.append(got)
            if records[-1] is None:
                records[-1] = got
    blend = call(
        functools.partial(last_blend_kernel, z, masks, [half_lines] * (len(records) - 1)),
        [shape((beams, beams), bf16)] * 2,
        records,
        [],
        1 << 18,
        "blend",
    )
    (turned,) = call(
        functools.partial(turn_kernel, z, per_block, places),
        [shape((2, block, beams), f32)],
        [array for have in arrays for array in have] + list(blend),
        [],
        flops,
        "turn",
    )
    return turned


def wide_turn(z, block, children, known):
    sub_count, rows, half = z.sub_count, z.rows, z.half
    if block % LANES == 0:
        line = children.reshape(sub_count, block // LANES, 2, rows, LANES).transpose(0, 2, 3, 1, 4)
    else:
        line = children.reshape(z.outer, 2, rows, LANES // block, block).transpose(0, 3, 1, 2, 4)
    gathered = lax.all_to_all(line.reshape(sub_count, 2 * rows, block), "sub", 0, 0, tiled=True)
    gathered = gathered.reshape(sub_count, 2, 2, half, block)
    table = known.reshape(z.blocks, z.record, z.slots, rows).transpose(0, 2, 1, 3)
    table = table.reshape(-1, z.record, rows)[:sub_count]
    weights = table[:, : z.at_offset].reshape(sub_count, 2, z.taps, rows)
    offsets = table[:, z.at_offset : z.at_shift].astype(jnp.int32)
    columns = jnp.arange(half, dtype=jnp.int32)
    stencil = 0.0
    for tap in range(z.taps):
        hits = columns == offsets[..., None] + tap
        stencil = stencil + jnp.where(hits, weights[:, :, tap, :, None], 0.0)
    index = jnp.arange(sub_count, dtype=jnp.int32)
    side = (index >> z.last & 1)[:, None, None, None]
    chosen = jnp.where(side == 0, gathered[:, :, 0], gathered[:, :, 1])
    crossing = gathered[index ^ (1 << z.last)]
    crossing = jnp.where(side == 0, crossing[:, :, 0], crossing[:, :, 1])
    both = jnp.concatenate([chosen, crossing], axis=2)
    matrix = jnp.moveaxis(stencil, 1, 2).reshape(sub_count, rows, rows)
    merged = jnp.einsum("ijm,ipmq->pqij", matrix, both, precision=lax.Precision.HIGHEST)
    return merged.reshape(2, block, sub_count * rows)


def solution(mesh):
    placed = (
        P(None, ("img", "sub"), None),
        P(None, "sub", None, None),
        P(None, "sub", None, None),
        P(None, "sub", None, None),
        P(None, "sub", None, None, None),
    )
    return jax.shard_map(
        body, mesh=mesh, in_specs=placed, out_specs=P(None, ("img", "sub"), None), check_vma=False
    )
```

```python
import functools
import math

import jax
import jax.numpy as jnp
import numpy as np
from jax import lax
from jax.experimental import pallas as pl
from jax.experimental.pallas import tpu as pltpu
from jax.sharding import PartitionSpec as P


LANES = 128
MXU = 256
CHUNK = 256
VMEM_GRANT = 12 << 20
f32 = jnp.float32
bf16 = jnp.bfloat16


def swapped(block, axis, stride):
    count = lax.axis_size(axis)
    route = []
    for low in range(count):
        high = low | 1 << stride
        if high != low and high < count:
            route += [(low, high), (high, low)]
    return lax.ppermute(block, axis, route)


def call(kernel, outs, ins, scratch, flops, after=(), space=pltpu.VMEM):
    moved = sum(math.prod(o.shape) * o.dtype.itemsize for o in outs)
    moved += sum(math.prod(i.shape) * i.dtype.itemsize for i in ins)
    count = len(ins)

    def run(*refs):
        kernel(*refs[:count], *refs[count + len(after) :])

    return pl.pallas_call(
        run,
        out_shape=outs,
        in_specs=[pl.BlockSpec(memory_space=space)] * count
        + [pl.BlockSpec(memory_space=pl.ANY)] * len(after),
        out_specs=[pl.BlockSpec(memory_space=pltpu.VMEM)] * len(outs),
        scratch_shapes=scratch,
        cost_estimate=pl.CostEstimate(flops=flops, bytes_accessed=moved, transcendentals=0),
        compiler_params=pltpu.CompilerParams(vmem_limit_bytes=VMEM_GRANT),
    )(*ins, *after)


def lane_matrix(direction, scale):
    k = np.arange(LANES)
    angle = direction * 2.0 * np.pi * (np.outer(k, k) % LANES) / LANES
    c, s = np.cos(angle) * scale, np.sin(angle) * scale
    full = np.block([[c, s], [-s, c]]).astype(np.float32)
    high = full.astype(bf16)
    low = (full - high.astype(np.float32)).astype(bf16)
    return high, low


def lane_twiddle(outer, direction):
    total = outer * LANES
    turns = np.outer(np.arange(outer), np.arange(LANES)) % total
    angle = direction * 2.0 * np.pi * turns / total
    return np.stack([np.cos(angle), np.sin(angle)]).astype(np.float32)


def times_constant(value, turn):
    real, imag = value
    turn = turn % 1.0
    if turn == 0.0:
        return value
    if turn == 0.5:
        return (-real, -imag)
    if turn == 0.25:
        return (-imag, real)
    if turn == 0.75:
        return (imag, -real)
    c, s = math.cos(2 * math.pi * turn), math.sin(2 * math.pi * turn)
    if abs(abs(c) - abs(s)) < 1e-12:
        r = abs(c)
        sc, ss = math.copysign(1, c), math.copysign(1, s)
        a = (real if sc > 0 else -real) - (imag if ss > 0 else -imag)
        b = (real if ss > 0 else -real) + (imag if sc > 0 else -imag)
        return (a * r, b * r)
    return (real * c - imag * s, real * s + imag * c)


def small_dft(values, direction):
    count = len(values)
    if count == 1:
        return values
    even = small_dft(values[0::2], direction)
    odd = small_dft(values[1::2], direction)
    first, second = [], []
    for k in range(count // 2):
        o = times_constant(odd[k], direction * k / count)
        e = even[k]
        first.append((e[0] + o[0], e[1] + o[1]))
        second.append((e[0] - o[0], e[1] - o[1]))
    return first + second


def split_factors(count):
    inner = 1 << ((count.bit_length() - 1) + 1) // 2
    return count // inner, inner


def staged_dft(count, direction, load, store, scratch):
    outer, inner = split_factors(count)
    for b in range(inner):
        got = small_dft([load(inner * a + b) for a in range(outer)], direction)
        for c in range(outer):
            value = times_constant(got[c], direction * b * c / count)
            scratch[0, c * inner + b] = value[0]
            scratch[1, c * inner + b] = value[1]
    for c in range(outer):
        line = [(scratch[0, c * inner + b], scratch[1, c * inner + b]) for b in range(inner)]
        got = small_dft(line, direction)
        for d in range(inner):
            store(c + outer * d, got[d])


def put_split(high_ref, low_ref, row, rows, value):
    for part in range(2):
        high = value[part].astype(bf16)
        low = (value[part] - high.astype(f32)).astype(bf16)
        high_ref[row : row + rows, part * LANES : (part + 1) * LANES] = high
        low_ref[row : row + rows, part * LANES : (part + 1) * LANES] = low


def dot3(left_high, left_low, right_high, right_low):
    def one(a, b):
        return jnp.dot(a, b, preferred_element_type=f32)

    return one(left_high, right_high) + (one(left_low, right_high) + one(left_high, right_low))


def put_halves(keep_ref, send_ref, bit, group, i, block, half):
    low, high = block[:half], block[half:]
    keep = jnp.where(bit == 0, low, high)
    send = jnp.where(bit == 0, high, low)
    for part in range(2):
        cut = slice(part * LANES, (part + 1) * LANES)
        keep_ref[part * group + i] = keep[:, cut]
        send_ref[part * group + i] = send[:, cut]


def cos_sin(turns, full):
    quarter = full // 4
    turns = turns & (full - 1)
    quadrant = (turns + quarter // 2) >> (quarter.bit_length() - 1)
    x = (turns - quadrant * quarter).astype(f32) * (2.0 * math.pi / full)
    y = x * x
    sine, cosine = 0.0, 0.0
    for term in (9, 7, 5, 3, 1):
        sine = sine * y + (-1.0) ** (term // 2) / math.factorial(term)
    for term in (10, 8, 6, 4, 2, 0):
        cosine = cosine * y + (-1.0) ** (term // 2) / math.factorial(term)
    sine = sine * x
    odd = (quadrant & 1) == 1
    first = jnp.where(odd, sine, cosine)
    second = jnp.where(odd, cosine, sine)
    first = jnp.where(((quadrant + 1) & 2) == 2, -first, first)
    return first, jnp.where((quadrant & 2) == 2, -second, second)


class Sizes:
    def __init__(self, rows, outer, taps, sub_count):
        self.rows, self.outer, self.taps, self.sub_count = rows, outer, taps, sub_count
        self.half = rows // 2
        self.levels = sub_count.bit_length() - 1
        self.last = self.levels - 1
        self.group = max(1, min(outer, CHUNK // rows))
        self.at_offset = 2 * taps
        self.at_shift = self.at_offset + 2
        self.at_phase = self.at_shift + 2
        self.record = -(-(self.at_phase + 2) // 8) * 8
        self.pages = -(-self.levels * self.record // LANES)
        self.slots = LANES // rows
        self.blocks = -(-sub_count // self.slots)
        self.chunks = outer // self.group
        self.last_page = self.last * self.record // LANES


def prepare(z, shift, phase, offset, weight, tabs, pack, lines):
    me = lax.axis_index("sub")
    lines[...] = jnp.zeros_like(lines)
    for level in range(z.levels):
        at = level * z.record
        for c in range(2):
            lines[at + c * z.taps : at + (c + 1) * z.taps, : z.rows] = weight[level, 0, c]
        at += z.at_offset
        lines[at : at + 2, : z.rows] = offset[level, 0].astype(f32)
        lines[at + 2 : at + 4, : z.half] = shift[level, 0].astype(f32)
        lines[at + 4 : at + 6, : z.half] = phase[level, 0]
    for page in range(z.pages):
        turned = lines[page * LANES : (page + 1) * LANES, :].T[: z.rows]
        tabs[:, page * LANES : (page + 1) * LANES] = turned
        if page == z.last_page:
            pack[: z.rows] = turned
    spread = lines[z.last * z.record : (z.last + 1) * z.record, :]
    step = z.rows
    while step < LANES:
        spread = spread + pltpu.roll(spread, step, 1)
        step *= 2
    slot = lax.broadcasted_iota(jnp.int32, spread.shape, 1) // z.rows
    for block in range(z.blocks):
        at = z.rows + block * z.record
        pack[at : at + z.record] = jnp.where(slot + block * z.slots == me, spread, 0.0)


def rotation(z, shifts, phases, near, far):
    full = 4 * z.outer * LANES
    shape = (z.rows, LANES)
    lane = lax.broadcasted_iota(jnp.int32, shape, 1)
    signed = z.outer * jnp.where(lane >= LANES // 2, lane - LANES, lane)
    shifts = jnp.broadcast_to(jnp.concatenate(shifts, axis=0), shape).astype(jnp.int32)
    phases = jnp.broadcast_to(jnp.concatenate(phases, axis=0), shape)
    c, s = cos_sin(shifts * signed, full)
    pc, ps = jnp.cos(phases), jnp.sin(phases)
    near[0] = pc * c + ps * s
    near[1] = ps * c - pc * s
    c, s = cos_sin(shifts * lane, full)
    far[0] = c
    far[1] = -s


def of_children(z, table, at):
    return [table[: z.half, at + c : at + c + 1] for c in range(2)]


def last_tables_kernel(z, pack, other, near, far):
    low = (lax.axis_index("sub") >> z.last & 1) == 0
    at = z.last * z.record - z.last_page * LANES
    both = []
    for row in (z.at_shift, z.at_phase):
        mine = of_children(z, pack, at + row)[0]
        their = of_children(z, other, at + row)[1]
        both.append([jnp.where(low, mine, their), jnp.where(low, their, mine)])
    rotation(z, *both, near, far)


def tables_kernel(z, tabs, near, far, wide_high, wide_low):
    for level in range(z.last):
        at = level * z.record
        shifts, phases = of_children(z, tabs, at + z.at_shift), of_children(z, tabs, at + z.at_phase)
        rotation(z, shifts, phases, near.at[level], far.at[level])
    size = z.group * z.rows
    shape = (z.rows, size)
    column = lax.broadcasted_iota(jnp.int32, shape, 1)
    beam = column % z.half
    child = (column // z.half) % 2
    block = column // z.rows
    for level in range(z.last):
        at = level * z.record
        wide = jnp.zeros(shape, f32)
        for c in range(2):
            first = tabs[:, at + z.at_offset + c : at + z.at_offset + c + 1].astype(jnp.int32)
            for tap in range(z.taps):
                hits = (beam == first + tap) & (child == c)
                wide += jnp.where(hits, tabs[:, at + c * z.taps + tap : at + c * z.taps + tap + 1], 0.0)
        for i in range(z.group):
            value = jnp.where(block == i, wide, 0.0)
            high = value.astype(bf16)
            wide_high[level, i * z.rows : (i + 1) * z.rows] = high
            wide_low[level, i * z.rows : (i + 1) * z.rows] = (value - high.astype(f32)).astype(bf16)


def last_blend_kernel(z, ours, theirs, blend_high, blend_low):
    tail = z.blocks * z.record
    known = ours[ours.shape[0] - tail :] + theirs[theirs.shape[0] - tail :]
    me = lax.axis_index("sub")
    beams = z.sub_count * z.rows
    for block in range(beams // LANES):
        table = known[block * z.record : (block + 1) * z.record]
        shape = (z.rows, LANES)
        row = lax.broadcasted_iota(jnp.int32, shape, 0)
        owner = lax.broadcasted_iota(jnp.int32, shape, 1) // z.rows + block * z.slots
        mine = (row // z.half) == (owner >> z.last & 1)
        parts = []
        for c in range(2):
            first = jnp.broadcast_to(table[z.at_offset + c : z.at_offset + c + 1].astype(jnp.int32), shape)
            total = jnp.zeros(shape, f32)
            for tap in range(z.taps):
                hits = (row % z.half == first + tap) & mine
                line = jnp.broadcast_to(table[c * z.taps + tap : c * z.taps + tap + 1], shape)
                total += jnp.where(hits, line, 0.0)
            parts.append(total)
        for away in range(z.sub_count):
            source = me ^ away
            value = jnp.where(owner == source, parts[0], 0.0)
            value = jnp.where(owner == (source ^ (1 << z.last)), parts[1], value)
            high = value.astype(bf16)
            at = (slice(away * z.rows, (away + 1) * z.rows), slice(block * LANES, (block + 1) * LANES))
            blend_high[at] = high
            blend_low[at] = (value - high.astype(f32)).astype(bf16)


def start_kernel(z, *refs):
    sources, refs = refs[:8], refs[8:]
    tabs, pack, refs = refs[0], refs[1], refs[2:]
    keeps, sends, refs = refs[: z.chunks], refs[z.chunks : 2 * z.chunks], refs[2 * z.chunks :]
    held, (lines, mid, high, low, sems) = refs[:8], refs[8:]
    copies = [
        pltpu.make_async_copy(source, place, sems.at[i])
        for i, (source, place) in enumerate(zip(sources, held))
    ]
    for copy in copies:
        copy.start()
    for copy in copies[:4]:
        copy.wait()
    prepare(z, *held[:4], tabs, pack, lines)
    image, twiddle, high_m, low_m = held[4:]
    copies[4].wait()
    copies[5].wait()

    def load(q):
        cut = slice(q * LANES, (q + 1) * LANES)
        return image[0, :, cut], image[1, :, cut]

    def store(k, value):
        c, s = twiddle[0, k : k + 1, :], twiddle[1, k : k + 1, :]
        value = (value[0] * c - value[1] * s, value[0] * s + value[1] * c)
        put_split(high, low, k * z.rows, z.rows, value)

    staged_dft(z.outer, -1, load, store, mid)
    bit = lax.axis_index("sub") & 1
    size = z.group * z.rows
    copies[6].wait()
    copies[7].wait()
    for g in range(z.chunks):
        cut = slice(g * size, (g + 1) * size)
        out = dot3(high[cut], low[cut], high_m[...], low_m[...])
        for i in range(z.group):
            block = out[i * z.rows : (i + 1) * z.rows]
            put_halves(keeps[g], sends[g], bit, z.group, i, block, z.half)


def rotated(value, near, far, k):
    shape = value[0].shape
    fr = jnp.broadcast_to(far[0][:, k : k + 1], shape)
    fi = jnp.broadcast_to(far[1][:, k : k + 1], shape)
    nr, ni = near[0], near[1]
    rr, ri = nr * fr - ni * fi, nr * fi + ni * fr
    return value[0] * rr - value[1] * ri, value[0] * ri + value[1] * rr


def blended(z, level, chunk, keep, arrived, near, far, wide_high, wide_low, high, low):
    close = near[level, 0], near[level, 1]
    steps = far[level, 0], far[level, 1]
    for i in range(z.group):
        value = tuple(
            jnp.concatenate([keep[part * z.group + i], arrived[part * z.group + i]], axis=0)
            for part in range(2)
        )
        value = rotated(value, close, steps, chunk * z.group + i)
        put_split(high, low, i * z.rows, z.rows, value)
    return dot3(wide_high[level], wide_low[level], high[...], low[...])


def level_kernel(z, level, chunk, riding, kept, arrived, *refs):
    packs, refs = refs[:riding], refs[riding:]
    near, far, wide_high, wide_low, keep, send, high, low = refs
    bit = lax.axis_index("sub") >> (level + 1) & 1
    out = blended(z, level, chunk, kept, arrived, near, far, wide_high, wide_low, high, low)
    for i in range(z.group):
        put_halves(keep, send, bit, z.group, i, out[i * z.rows : (i + 1) * z.rows], z.half)
    if riding:
        known = packs[0][z.rows :] + packs[1][z.rows :]
        send[2 * z.group :] = known.reshape(-1, z.half, LANES)


def return_kernel(
    z, chunk, kept, arrived, near, far, wide_high, wide_low, last_near, last_far,
    high_m, low_m, twiddle, back, high, low,
):
    out = blended(z, z.last - 1, chunk, kept, arrived, near, far, wide_high, wide_low, high, low)
    close = last_near[0], last_near[1]
    steps = last_far[0], last_far[1]
    for i in range(z.group):
        block = out[i * z.rows : (i + 1) * z.rows]
        value = rotated((block[:, :LANES], block[:, LANES:]), close, steps, chunk * z.group + i)
        put_split(high, low, i * z.rows, z.rows, value)
    out = dot3(high[...], low[...], high_m[...], low_m[...])
    for i in range(z.group):
        k = chunk * z.group + i
        block = out[i * z.rows : (i + 1) * z.rows]
        real, imag = block[:, :LANES], block[:, LANES:]
        c, s = twiddle[0, k : k + 1, :], twiddle[1, k : k + 1, :]
        back[0, i] = real * c - imag * s
        back[1, i] = real * s + imag * c


def gather_back(z, backs, store, mid):
    def load(k):
        back, i = backs[k // z.group], k % z.group
        return back[0, i], back[1, i]

    staged_dft(z.outer, 1, load, store, mid)


def ranges_kernel(z, *refs):
    backs, out_ref, mid = refs[: z.chunks], refs[z.chunks], refs[z.chunks + 1]

    def store(q, value):
        for part in range(2):
            out_ref[q, part] = value[part]

    gather_back(z, backs, store, mid)


def deal_kernel(z, per_block, riding, *refs):
    pairs = z.sub_count // 2
    lines = 2 * per_block * z.rows
    backs, refs = refs[: z.chunks], refs[z.chunks :]
    sent, arrived, refs = refs[0], refs[1], refs[2:]
    outs, (records, mid, whole) = refs[:pairs], refs[pairs:]

    def store(q, value):
        for part in range(2):
            at = (part * per_block + q % per_block) * z.rows
            whole[q // per_block, at : at + z.rows] = value[part]

    gather_back(z, backs, store, mid)
    me = lax.axis_index("sub")
    for k in range(pairs):
        for side in range(2):
            outs[k][side * lines : (side + 1) * lines] = whole[me ^ (2 * k + side)]
    known = (sent[2 * z.group :] + arrived[2 * z.group :]).reshape(-1, LANES)
    records[...] = known
    if riding:
        outs[1][2 * lines :] = known


def stack_kernel(lines, count, *refs):
    for i, ref in enumerate(refs[:count]):
        refs[-1][i * lines : (i + 1) * lines] = ref[lines : 2 * lines]
    if len(refs) > count + 1:
        known = refs[count][...]
        for ref in refs[count + 1 : -1]:
            known = known + ref[2 * lines :]
        refs[-1][count * lines :] = known


def turn_kernel(z, per_block, places, *refs):
    blend_high, blend_low, out_ref = refs[-3:]
    for part in range(2 * per_block):
        line = []
        for array, at in places:
            at += part * z.rows
            line.append(refs[array][at : at + z.rows])
        line = jnp.concatenate(line, axis=0).T
        high = line.astype(bf16)
        low = (line - high.astype(f32)).astype(bf16)
        a, cut = part // per_block, part % per_block
        out_ref[a, cut * LANES : (cut + 1) * LANES, :] = dot3(high, low, blend_high[...], blend_low[...])


def pair_order(pairs):
    return [*range(pairs // 2, pairs), *range(1, pairs // 2)]


def body(sub_images, shift_table, phase_table, offset_table, weight_table):
    _, rows, range_bins = sub_images.shape
    outer = range_bins // LANES
    sub_count = lax.axis_size("sub")
    z = Sizes(rows, outer, weight_table.shape[3], sub_count)
    size = z.group * rows
    flops = 3 * 2 * size * MXU * MXU
    shape = jax.ShapeDtypeStruct
    mid = pltpu.VMEM((2, outer, rows, LANES), f32)
    halves = [pltpu.VMEM((size, 2 * LANES), bf16)] * 2
    slab = shape((2 * z.group, z.half, LANES), f32)

    sources = [shift_table, phase_table, offset_table, weight_table, sub_images]
    sources += [jnp.asarray(table) for table in (lane_twiddle(outer, -1), *lane_matrix(-1, 1.0))]
    sources = [pltpu.with_memory_space_constraint(source, pltpu.HBM) for source in sources]
    tabs, pack, *parts = call(
        functools.partial(start_kernel, z),
        [shape((rows, z.pages * LANES), f32), shape((rows + z.blocks * z.record, LANES), f32)]
        + [slab] * (2 * z.chunks),
        sources,
        [pltpu.VMEM(source.shape, source.dtype) for source in sources]
        + [pltpu.VMEM((z.pages * LANES, LANES), f32), mid]
        + [pltpu.VMEM((outer * rows, 2 * LANES), bf16)] * 2
        + [pltpu.SemaphoreType.DMA((len(sources),))],
        flops * z.chunks,
        space=pltpu.HBM,
    )
    keeps, sends = parts[: z.chunks], parts[z.chunks :]
    arrived = [swapped(send, "sub", 0) for send in sends]
    tables = call(
        functools.partial(tables_kernel, z),
        [shape((z.last, 2, rows, LANES), f32)] * 2 + [shape((z.last, size, size), bf16)] * 2,
        [tabs],
        [],
        1 << 20,
    )
    other = swapped(pack, "sub", z.last)
    tail = z.blocks * z.record
    longer = shape((2 * z.group + tail // z.half, z.half, LANES), f32)
    for level in range(z.last - 1):
        for chunk in range(z.chunks):
            rides = level == z.last - 2 and chunk == z.chunks - 1
            keeps[chunk], sends[chunk] = call(
                functools.partial(level_kernel, z, level, chunk, 2 * rides),
                [slab, longer if rides else slab],
                [keeps[chunk], arrived[chunk]] + [pack, other] * rides + list(tables),
                halves,
                flops,
            )
            arrived[chunk] = swapped(sends[chunk], "sub", level + 1)
    last_tables = call(
        functools.partial(last_tables_kernel, z),
        [shape((2, rows, LANES), f32)] * 2,
        [pack, other],
        [],
        1 << 16,
    )
    way_back = [*lane_matrix(1, 1.0 / range_bins), lane_twiddle(outer, 1)]
    backs = [
        call(
            functools.partial(return_kernel, z, chunk),
            [shape((2, z.group, rows, LANES), f32)],
            [keeps[chunk], arrived[chunk], *tables, *last_tables, *way_back],
            halves,
            2 * flops,
        )[0]
        for chunk in range(z.chunks)
    ]
    block = range_bins // sub_count
    beams = sub_count * rows
    if block % LANES or beams > MXU or sub_count < 8:
        (children,) = call(
            functools.partial(ranges_kernel, z),
            [shape((outer, 2, rows, LANES), f32)],
            backs,
            [mid],
            flops,
        )
        known = (sends[-1] + arrived[-1])[2 * z.group :].reshape(-1, LANES)
        for level in range(z.last - 1):
            known = known + swapped(known, "sub", level)
        return wide_turn(z, block, children, known)

    per_block = block // LANES
    pairs = sub_count // 2
    lines = 2 * per_block * rows
    riding = z.last > 2
    *messages, known = call(
        functools.partial(deal_kernel, z, per_block, riding),
        [shape((2 * lines + (tail if riding and k == 1 else 0), LANES), f32) for k in range(pairs)]
        + [shape((tail, LANES), f32)],
        [*backs, sends[-1], arrived[-1]],
        [mid, pltpu.VMEM((sub_count, lines, LANES), f32)],
        flops,
    )
    arrays = [messages[0]] + [None] * (pairs - 1)
    for k in pair_order(pairs):
        route = [(i, i ^ (2 * k)) for i in range(sub_count)]
        arrays[k] = lax.ppermute(messages[k], "sub", route)
    places = {2 * k: (k, 0) for k in range(pairs)}
    cuts = [list(range(pairs // 2)), list(range(pairs // 2, pairs))]
    crossing = []
    for cut in cuts:
        records = [] if crossing else [known] + [arrays[1]] * riding
        (both,) = call(
            functools.partial(stack_kernel, lines, len(cut)),
            [shape((len(cut) * lines + tail * bool(records), LANES), f32)],
            [arrays[k] for k in cut] + records,
            [],
            1,
        )
        places.update({2 * k + 1: (len(arrays), i * lines) for i, k in enumerate(cut)})
        crossing.append(both)
        arrays.append(swapped(both, "sub", 0))
    blend = call(
        functools.partial(last_blend_kernel, z),
        [shape((beams, beams), bf16)] * 2,
        [crossing[0], arrays[pairs]],
        [],
        1 << 18,
    )
    (turned,) = call(
        functools.partial(turn_kernel, z, per_block, [places[away] for away in range(sub_count)]),
        [shape((2, block, beams), f32)],
        [*arrays, *blend],
        [],
        flops,
    )
    return turned


def wide_turn(z, block, children, known):
    sub_count, rows, half = z.sub_count, z.rows, z.half
    if block % LANES == 0:
        line = children.reshape(sub_count, block // LANES, 2, rows, LANES).transpose(0, 2, 3, 1, 4)
    else:
        line = children.reshape(z.outer, 2, rows, LANES // block, block).transpose(0, 3, 1, 2, 4)
    gathered = lax.all_to_all(line.reshape(sub_count, 2 * rows, block), "sub", 0, 0, tiled=True)
    gathered = gathered.reshape(sub_count, 2, 2, half, block)
    table = known.reshape(z.blocks, z.record, z.slots, rows).transpose(0, 2, 1, 3)
    table = table.reshape(-1, z.record, rows)[:sub_count]
    weights = table[:, : z.at_offset].reshape(sub_count, 2, z.taps, rows)
    offsets = table[:, z.at_offset : z.at_shift].astype(jnp.int32)
    columns = jnp.arange(half, dtype=jnp.int32)
    stencil = 0.0
    for tap in range(z.taps):
        hits = columns == offsets[..., None] + tap
        stencil = stencil + jnp.where(hits, weights[:, :, tap, :, None], 0.0)
    index = jnp.arange(sub_count, dtype=jnp.int32)
    side = (index >> z.last & 1)[:, None, None, None]
    chosen = jnp.where(side == 0, gathered[:, :, 0], gathered[:, :, 1])
    crossing = gathered[index ^ (1 << z.last)]
    crossing = jnp.where(side == 0, crossing[:, :, 0], crossing[:, :, 1])
    both = jnp.concatenate([chosen, crossing], axis=2)
    matrix = jnp.moveaxis(stencil, 1, 2).reshape(sub_count, rows, rows)
    merged = jnp.einsum("ijm,ipmq->pqij", matrix, both, precision=lax.Precision.HIGHEST)
    return merged.reshape(2, block, sub_count * rows)


def solution(mesh):
    placed = (
        P(None, ("img", "sub"), None),
        P(None, "sub", None, None),
        P(None, "sub", None, None),
        P(None, "sub", None, None),
        P(None, "sub", None, None, None),
    )

    return jax.shard_map(
        body, mesh=mesh, in_specs=placed, out_specs=P(None, ("img", "sub"), None), check_vma=False
    )
```

```python
import functools
import math

import jax
import jax.numpy as jnp
import numpy as np
from jax import lax
from jax.experimental import pallas as pl
from jax.experimental.pallas import tpu as pltpu
from jax.sharding import PartitionSpec as P


LANES = 128
MXU = 256
CHUNK = 256
VMEM_GRANT = 12 << 20
f32 = jnp.float32
bf16 = jnp.bfloat16


def swapped(block, axis, stride):
    count = lax.axis_size(axis)
    route = []
    for low in range(count):
        high = low | 1 << stride
        if high != low and high < count:
            route += [(low, high), (high, low)]
    return lax.ppermute(block, axis, route)


def call(kernel, outs, ins, scratch, flops, space=pltpu.VMEM, out_space=pltpu.VMEM):
    moved = sum(math.prod(o.shape) * o.dtype.itemsize for o in outs)
    moved += sum(math.prod(i.shape) * i.dtype.itemsize for i in ins)
    return pl.pallas_call(
        kernel,
        out_shape=outs,
        in_specs=[pl.BlockSpec(memory_space=space)] * len(ins),
        out_specs=[pl.BlockSpec(memory_space=out_space)] * len(outs),
        scratch_shapes=scratch,
        cost_estimate=pl.CostEstimate(flops=flops, bytes_accessed=moved, transcendentals=0),
        compiler_params=pltpu.CompilerParams(vmem_limit_bytes=VMEM_GRANT),
    )(*ins)


def lane_matrix(direction, scale):
    k = np.arange(LANES)
    angle = direction * 2.0 * np.pi * (np.outer(k, k) % LANES) / LANES
    c, s = np.cos(angle) * scale, np.sin(angle) * scale
    full = np.block([[c, s], [-s, c]]).astype(np.float32)
    high = full.astype(bf16)
    low = (full - high.astype(np.float32)).astype(bf16)
    return high, low


def lane_twiddle(outer, direction):
    total = outer * LANES
    turns = np.outer(np.arange(outer), np.arange(LANES)) % total
    angle = direction * 2.0 * np.pi * turns / total
    return np.stack([np.cos(angle), np.sin(angle)]).astype(np.float32)


def times_constant(value, turn):
    real, imag = value
    turn = turn % 1.0
    if turn == 0.0:
        return value
    if turn == 0.5:
        return (-real, -imag)
    if turn == 0.25:
        return (-imag, real)
    if turn == 0.75:
        return (imag, -real)
    c, s = math.cos(2 * math.pi * turn), math.sin(2 * math.pi * turn)
    if abs(abs(c) - abs(s)) < 1e-12:
        r = abs(c)
        sc, ss = math.copysign(1, c), math.copysign(1, s)
        a = (real if sc > 0 else -real) - (imag if ss > 0 else -imag)
        b = (real if ss > 0 else -real) + (imag if sc > 0 else -imag)
        return (a * r, b * r)
    return (real * c - imag * s, real * s + imag * c)


def small_dft(values, direction):
    count = len(values)
    if count == 1:
        return values
    even = small_dft(values[0::2], direction)
    odd = small_dft(values[1::2], direction)
    first, second = [], []
    for k in range(count // 2):
        o = times_constant(odd[k], direction * k / count)
        e = even[k]
        first.append((e[0] + o[0], e[1] + o[1]))
        second.append((e[0] - o[0], e[1] - o[1]))
    return first + second


def split_factors(count):
    inner = 1 << ((count.bit_length() - 1) + 1) // 2
    return count // inner, inner


def staged_dft(count, direction, load, store, scratch):
    outer, inner = split_factors(count)
    for b in range(inner):
        got = small_dft([load(inner * a + b) for a in range(outer)], direction)
        for c in range(outer):
            value = times_constant(got[c], direction * b * c / count)
            scratch[0, c * inner + b] = value[0]
            scratch[1, c * inner + b] = value[1]
    for c in range(outer):
        line = [(scratch[0, c * inner + b], scratch[1, c * inner + b]) for b in range(inner)]
        got = small_dft(line, direction)
        for d in range(inner):
            store(c + outer * d, got[d])


def put_split(high_ref, low_ref, row, rows, value):
    for part in range(2):
        high = value[part].astype(bf16)
        low = (value[part] - high.astype(f32)).astype(bf16)
        high_ref[row : row + rows, part * LANES : (part + 1) * LANES] = high
        low_ref[row : row + rows, part * LANES : (part + 1) * LANES] = low


def dot3(left_high, left_low, right_high, right_low):
    def one(a, b):
        return jnp.dot(a, b, preferred_element_type=f32)

    return one(left_high, right_high) + (one(left_low, right_high) + one(left_high, right_low))


def put_halves(keep_ref, send_ref, bit, group, i, block, half):
    low, high = block[:half], block[half:]
    keep = jnp.where(bit == 0, low, high)
    send = jnp.where(bit == 0, high, low)
    for part in range(2):
        cut = slice(part * LANES, (part + 1) * LANES)
        keep_ref[part * group + i] = keep[:, cut]
        send_ref[part * group + i] = send[:, cut]


def cos_sin(turns, full):
    quarter = full // 4
    turns = turns & (full - 1)
    quadrant = (turns + quarter // 2) >> (quarter.bit_length() - 1)
    x = (turns - quadrant * quarter).astype(f32) * (2.0 * math.pi / full)
    y = x * x
    sine, cosine = 0.0, 0.0
    for term in (9, 7, 5, 3, 1):
        sine = sine * y + (-1.0) ** (term // 2) / math.factorial(term)
    for term in (10, 8, 6, 4, 2, 0):
        cosine = cosine * y + (-1.0) ** (term // 2) / math.factorial(term)
    sine = sine * x
    odd = (quadrant & 1) == 1
    first = jnp.where(odd, sine, cosine)
    second = jnp.where(odd, cosine, sine)
    first = jnp.where(((quadrant + 1) & 2) == 2, -first, first)
    return first, jnp.where((quadrant & 2) == 2, -second, second)


class Sizes:
    def __init__(self, rows, outer, taps, sub_count):
        self.rows, self.outer, self.taps, self.sub_count = rows, outer, taps, sub_count
        self.half = rows // 2
        self.levels = sub_count.bit_length() - 1
        self.last = self.levels - 1
        self.group = max(1, min(outer, CHUNK // rows))
        self.at_offset = 2 * taps
        self.at_shift = self.at_offset + 2
        self.at_phase = self.at_shift + 2
        self.record = -(-(self.at_phase + 2) // 8) * 8
        self.pages = -(-self.levels * self.record // LANES)
        self.slots = LANES // rows
        self.blocks = -(-sub_count // self.slots)
        self.chunks = outer // self.group
        self.last_page = self.last * self.record // LANES


def prepare(z, shift, phase, offset, weight, tabs, pack, lines):
    me = lax.axis_index("sub")
    lines[...] = jnp.zeros_like(lines)
    for level in range(z.levels):
        at = level * z.record
        for c in range(2):
            lines[at + c * z.taps : at + (c + 1) * z.taps, : z.rows] = weight[level, 0, c]
        at += z.at_offset
        lines[at : at + 2, : z.rows] = offset[level, 0].astype(f32)
        lines[at + 2 : at + 4, : z.half] = shift[level, 0].astype(f32)
        lines[at + 4 : at + 6, : z.half] = phase[level, 0]
    for page in range(z.pages):
        turned = lines[page * LANES : (page + 1) * LANES, :].T[: z.rows]
        tabs[:, page * LANES : (page + 1) * LANES] = turned
        if page == z.last_page:
            pack[: z.rows] = turned
    spread = lines[z.last * z.record : (z.last + 1) * z.record, :]
    step = z.rows
    while step < LANES:
        spread = spread + pltpu.roll(spread, step, 1)
        step *= 2
    slot = lax.broadcasted_iota(jnp.int32, spread.shape, 1) // z.rows
    for block in range(z.blocks):
        at = z.rows + block * z.record
        pack[at : at + z.record] = jnp.where(slot + block * z.slots == me, spread, 0.0)


def rotation(z, shifts, phases, near, far):
    full = 4 * z.outer * LANES
    shape = (z.rows, LANES)
    lane = lax.broadcasted_iota(jnp.int32, shape, 1)
    signed = z.outer * jnp.where(lane >= LANES // 2, lane - LANES, lane)
    shifts = jnp.broadcast_to(jnp.concatenate(shifts, axis=0), shape).astype(jnp.int32)
    phases = jnp.broadcast_to(jnp.concatenate(phases, axis=0), shape)
    c, s = cos_sin(shifts * signed, full)
    pc, ps = jnp.cos(phases), jnp.sin(phases)
    near[0] = pc * c + ps * s
    near[1] = ps * c - pc * s
    c, s = cos_sin(shifts * lane, full)
    far[0] = c
    far[1] = -s


def of_children(z, table, at):
    return [table[: z.half, at + c : at + c + 1] for c in range(2)]


def last_tables_kernel(z, pack, other, near, far):
    low = (lax.axis_index("sub") >> z.last & 1) == 0
    at = z.last * z.record - z.last_page * LANES
    both = []
    for row in (z.at_shift, z.at_phase):
        mine = of_children(z, pack, at + row)[0]
        their = of_children(z, other, at + row)[1]
        both.append([jnp.where(low, mine, their), jnp.where(low, their, mine)])
    rotation(z, *both, near, far)


def tables_kernel(z, tabs, near, far, wide_high, wide_low):
    for level in range(z.last):
        at = level * z.record
        shifts, phases = of_children(z, tabs, at + z.at_shift), of_children(z, tabs, at + z.at_phase)
        rotation(z, shifts, phases, near.at[level], far.at[level])
    size = z.group * z.rows
    shape = (z.rows, size)
    column = lax.broadcasted_iota(jnp.int32, shape, 1)
    beam = column % z.half
    child = (column // z.half) % 2
    block = column // z.rows
    for level in range(z.last):
        at = level * z.record
        wide = jnp.zeros(shape, f32)
        for c in range(2):
            first = tabs[:, at + z.at_offset + c : at + z.at_offset + c + 1].astype(jnp.int32)
            for tap in range(z.taps):
                hits = (beam == first + tap) & (child == c)
                wide += jnp.where(hits, tabs[:, at + c * z.taps + tap : at + c * z.taps + tap + 1], 0.0)
        for i in range(z.group):
            value = jnp.where(block == i, wide, 0.0)
            high = value.astype(bf16)
            wide_high[level, i * z.rows : (i + 1) * z.rows] = high
            wide_low[level, i * z.rows : (i + 1) * z.rows] = (value - high.astype(f32)).astype(bf16)


def last_blend_kernel(z, order, ours, theirs, blend_high, blend_low):
    tail = z.blocks * z.record
    known = ours[ours.shape[0] - tail :] + theirs[theirs.shape[0] - tail :]
    me = lax.axis_index("sub")
    beams = z.sub_count * z.rows
    for block in range(beams // LANES):
        table = known[block * z.record : (block + 1) * z.record]
        shape = (z.rows, LANES)
        row = lax.broadcasted_iota(jnp.int32, shape, 0)
        owner = lax.broadcasted_iota(jnp.int32, shape, 1) // z.rows + block * z.slots
        mine = (row // z.half) == (owner >> z.last & 1)
        parts = []
        for c in range(2):
            first = jnp.broadcast_to(table[z.at_offset + c : z.at_offset + c + 1].astype(jnp.int32), shape)
            total = jnp.zeros(shape, f32)
            for tap in range(z.taps):
                hits = (row % z.half == first + tap) & mine
                line = jnp.broadcast_to(table[c * z.taps + tap : c * z.taps + tap + 1], shape)
                total += jnp.where(hits, line, 0.0)
            parts.append(total)
        for i, away in enumerate(order):
            source = me ^ away
            value = jnp.where(owner == source, parts[0], 0.0)
            value = jnp.where(owner == (source ^ (1 << z.last)), parts[1], value)
            high = value.astype(bf16)
            at = (slice(i * z.rows, (i + 1) * z.rows), slice(block * LANES, (block + 1) * LANES))
            blend_high[at] = high
            blend_low[at] = (value - high.astype(f32)).astype(bf16)


def forward(z, load, keep, mid, high, low, high_m, low_m, twiddle):
    held = []

    def store(k, value):
        c, s = twiddle[0, k : k + 1, :], twiddle[1, k : k + 1, :]
        held.append((k, (value[0] * c - value[1] * s, value[0] * s + value[1] * c)))
        if len(held) % 2 == 0:
            pair = tuple(jnp.concatenate([held[-2][1][p], held[-1][1][p]], axis=0) for p in range(2))
            put_split(high, low, (len(held) - 2) * z.half, 2 * z.half, pair)

    staged_dft(z.outer, -1, load, store, mid)
    out = dot3(high[...], low[...], high_m, low_m)
    for i, (k, _) in enumerate(held):
        for part in range(2):
            keep[part * z.outer + k] = out[i * z.half : (i + 1) * z.half, part * LANES : (part + 1) * LANES]


def start_kernel(z, *refs):
    sources, refs = refs[:8], refs[8:]
    tabs, pack, keep, refs = refs[0], refs[1], refs[2], refs[3:]
    held, (lines, mid, high, low, sems) = refs[:8], refs[8:]
    bit = lax.axis_index("sub") & 1
    rows = pl.ds(pl.multiple_of(bit * z.half, z.half), z.half)
    sources = [*sources[:4], sources[4].at[:, rows], *sources[5:]]
    copies = [
        pltpu.make_async_copy(source, place, sems.at[i])
        for i, (source, place) in enumerate(zip(sources, held))
    ]
    for copy in copies:
        copy.start()
    for copy in copies[:4]:
        copy.wait()
    prepare(z, *held[:4], tabs, pack, lines)
    image, twiddle, high_m, low_m = held[4:]
    for copy in copies[4:]:
        copy.wait()

    def load(q):
        cut = slice(q * LANES, (q + 1) * LANES)
        return image[0, :, cut], image[1, :, cut]

    forward(z, load, keep, mid, high, low, high_m[...], low_m[...], twiddle)


def join_kernel(z, image, twiddle, high_m, low_m, kept, near, far, wide_high, wide_low, keep, send, spectrum, mid, high, low):
    bit = lax.axis_index("sub") & 1
    rows = pl.ds(pl.multiple_of(bit * z.half, z.half), z.half)

    def load(q):
        cut = slice(q * LANES, (q + 1) * LANES)
        return image[0, rows, cut], image[1, rows, cut]

    forward(z, load, spectrum, mid, high, low, high_m[...], low_m[...], twiddle)
    level_kernel(z, 0, 0, 0, z.outer, kept, spectrum, near, far, wide_high, wide_low, keep, send, high, low)


def rotated(value, near, far, k):
    shape = value[0].shape
    fr = jnp.broadcast_to(far[0][:, k : k + 1], shape)
    fi = jnp.broadcast_to(far[1][:, k : k + 1], shape)
    nr, ni = near[0], near[1]
    rr, ri = nr * fr - ni * fi, nr * fi + ni * fr
    return value[0] * rr - value[1] * ri, value[0] * ri + value[1] * rr


def blended(z, level, chunk, stride, keep, arrived, near, far, wide_high, wide_low, high, low):
    close = near[level, 0], near[level, 1]
    steps = far[level, 0], far[level, 1]
    for i in range(z.group):
        spots = [part * z.group + i for part in range(2)]
        if stride:
            spots = [part * stride + chunk * z.group + i for part in range(2)]
        value = tuple(jnp.concatenate([keep[spot], arrived[spot]], axis=0) for spot in spots)
        value = rotated(value, close, steps, chunk * z.group + i)
        put_split(high, low, i * z.rows, z.rows, value)
    return dot3(wide_high[level], wide_low[level], high[...], low[...])


def level_kernel(z, level, chunk, riding, stride, kept, arrived, *refs):
    packs, refs = refs[:riding], refs[riding:]
    near, far, wide_high, wide_low, keep, send, high, low = refs
    bit = lax.axis_index("sub") >> (level + 1) & 1
    out = blended(z, level, chunk, stride, kept, arrived, near, far, wide_high, wide_low, high, low)
    for i in range(z.group):
        put_halves(keep, send, bit, z.group, i, out[i * z.rows : (i + 1) * z.rows], z.half)
    if riding:
        known = packs[0][z.rows :] + packs[1][z.rows :]
        send[2 * z.group :] = known.reshape(-1, z.half, LANES)


def return_kernel(
    z, chunk, kept, arrived, near, far, wide_high, wide_low, last_near, last_far,
    high_m, low_m, twiddle, back, high, low,
):
    out = blended(z, z.last - 1, chunk, 0, kept, arrived, near, far, wide_high, wide_low, high, low)
    close = last_near[0], last_near[1]
    steps = last_far[0], last_far[1]
    for i in range(z.group):
        block = out[i * z.rows : (i + 1) * z.rows]
        value = rotated((block[:, :LANES], block[:, LANES:]), close, steps, chunk * z.group + i)
        put_split(high, low, i * z.rows, z.rows, value)
    out = dot3(high[...], low[...], high_m[...], low_m[...])
    for i in range(z.group):
        k = chunk * z.group + i
        block = out[i * z.rows : (i + 1) * z.rows]
        real, imag = block[:, :LANES], block[:, LANES:]
        c, s = twiddle[0, k : k + 1, :], twiddle[1, k : k + 1, :]
        back[0, i] = real * c - imag * s
        back[1, i] = real * s + imag * c


def gather_back(z, backs, store, mid):
    def load(k):
        back, i = backs[k // z.group], k % z.group
        return back[0, i], back[1, i]

    staged_dft(z.outer, 1, load, store, mid)


def ranges_kernel(z, *refs):
    backs, out_ref, mid = refs[: z.chunks], refs[z.chunks], refs[z.chunks + 1]

    def store(q, value):
        for part in range(2):
            out_ref[q, part] = value[part]

    gather_back(z, backs, store, mid)


def deal_kernel(z, per_block, messages, riding, *refs):
    lines = 2 * per_block * z.rows
    backs, refs = refs[: z.chunks], refs[z.chunks :]
    sent, arrived, refs = refs[0], refs[1], refs[2:]
    outs, (records, mid, whole) = refs[: len(messages)], refs[len(messages) :]

    def store(q, value):
        for part in range(2):
            at = (part * per_block + q % per_block) * z.rows
            whole[q // per_block, at : at + z.rows] = value[part]

    gather_back(z, backs, store, mid)
    me = lax.axis_index("sub")
    for out, aways in zip(outs, messages):
        for i, away in enumerate(aways):
            out[i * lines : (i + 1) * lines] = whole[me ^ away]
    known = (sent[2 * z.group :] + arrived[2 * z.group :]).reshape(-1, LANES)
    records[...] = known
    if riding is not None:
        outs[riding][2 * lines :] = known


def stack_kernel(lines, count, *refs):
    for i, ref in enumerate(refs[:count]):
        refs[-1][i * lines : (i + 1) * lines] = ref[lines : 2 * lines]
    if len(refs) > count + 1:
        known = refs[count][...]
        for ref in refs[count + 1 : -1]:
            known = known + ref[2 * lines :]
        refs[-1][count * lines :] = known


def turn_kernel(z, per_block, places, first, adding, *refs):
    scratch = refs[len(refs) - 2 * adding :]
    refs = refs[: len(refs) - 2 * adding]
    blend_high, blend_low, *partial, out_ref = refs[len(refs) - 3 - adding :]
    size = len(places) * z.rows
    cut = slice(first, first + size)
    copies = []
    for part in range(2 * per_block):
        line = []
        for array, at in places:
            at += part * z.rows
            line.append(refs[array][at : at + z.rows])
        line = jnp.concatenate(line, axis=0).T
        high = line.astype(bf16)
        low = (line - high.astype(f32)).astype(bf16)
        total = dot3(high, low, blend_high[cut], blend_low[cut])
        at = (part // per_block, slice(part % per_block * LANES, (part % per_block + 1) * LANES))
        if adding:
            ready, sems = scratch
            ready[at] = total + partial[0][at]
            copies.append(pltpu.make_async_copy(ready.at[at], out_ref.at[at], sems.at[part]))
            copies[-1].start()
        else:
            out_ref[at] = total
    for copy in copies:
        copy.wait()


def pair_order(pairs):
    order = []
    for k in [*range(pairs // 2, pairs), *range(1, pairs // 2)]:
        order += [(2 * k,), (2 * k + 1,)] if k in [] else [(2 * k, 2 * k + 1)]
    return order


def body(sub_images, shift_table, phase_table, offset_table, weight_table):
    _, rows, range_bins = sub_images.shape
    outer = range_bins // LANES
    sub_count = lax.axis_size("sub")
    z = Sizes(rows, outer, weight_table.shape[3], sub_count)
    size = z.group * rows
    flops = 3 * 2 * size * MXU * MXU
    shape = jax.ShapeDtypeStruct
    mid = pltpu.VMEM((2, outer, rows, LANES), f32)
    halves = [pltpu.VMEM((size, 2 * LANES), bf16)] * 2
    slab = shape((2 * z.group, z.half, LANES), f32)

    def swap(send, level):
        return swapped(send, "sub", level)

    raw = swap(sub_images, 0)
    constants = [jnp.asarray(table) for table in (lane_twiddle(outer, -1), *lane_matrix(-1, 1.0))]
    sources = [shift_table, phase_table, offset_table, weight_table, sub_images, *constants]
    sources = [pltpu.with_memory_space_constraint(source, pltpu.HBM) for source in sources]
    spectra = shape((2 * outer, z.half, LANES), f32)
    small = pltpu.VMEM((2, outer, z.half, LANES), f32)
    places = [source.shape for source in sources]
    places[4] = (2, z.half, range_bins)
    tabs, pack, kept = call(
        functools.partial(start_kernel, z),
        [shape((rows, z.pages * LANES), f32), shape((rows + z.blocks * z.record, LANES), f32), spectra],
        sources,
        [pltpu.VMEM(place, source.dtype) for place, source in zip(places, sources)]
        + [pltpu.VMEM((z.pages * LANES, LANES), f32), small]
        + [pltpu.VMEM((outer * z.half, 2 * LANES), bf16)] * 2
        + [pltpu.SemaphoreType.DMA((len(sources),))],
        flops * z.chunks // 2,
        space=pltpu.HBM,
    )
    tables = call(
        functools.partial(tables_kernel, z),
        [shape((z.last, 2, rows, LANES), f32)] * 2 + [shape((z.last, size, size), bf16)] * 2,
        [tabs],
        [],
        1 << 20,
    )
    keep, send, spectrum = call(
        functools.partial(join_kernel, z),
        [slab, slab, spectra],
        [raw, *constants, kept, *tables],
        [small] + [pltpu.VMEM((outer * z.half, 2 * LANES), bf16)] * 2,
        flops * (1 + z.chunks // 2),
    )
    keeps, sends = [kept] * z.chunks, [None] * z.chunks
    arrived = [spectrum] * z.chunks
    keeps[0], sends[0], arrived[0] = keep, send, swap(send, 1)

    other = swapped(pack, "sub", z.last)
    tail = z.blocks * z.record
    longer = shape((2 * z.group + tail // z.half, z.half, LANES), f32)
    for level in range(z.last - 1):
        for chunk in range(0 if level else 1, z.chunks):
            rides = level == z.last - 2 and chunk == z.chunks - 1
            keeps[chunk], sends[chunk] = call(
                functools.partial(level_kernel, z, level, chunk, 2 * rides, 0 if level else z.outer),
                [slab, longer if rides else slab],
                [keeps[chunk], arrived[chunk]] + [pack, other] * rides + list(tables),
                halves,
                flops,
            )
            arrived[chunk] = swap(sends[chunk], level + 1)
    last_tables = call(
        functools.partial(last_tables_kernel, z), [shape((2, rows, LANES), f32)] * 2, [pack, other], [], 1 << 16
    )
    way_back = [*lane_matrix(1, 1.0 / range_bins), lane_twiddle(outer, 1)]
    backs = [
        call(
            functools.partial(return_kernel, z, chunk),
            [shape((2, z.group, rows, LANES), f32)],
            [keeps[chunk], arrived[chunk], *tables, *last_tables, *way_back],
            halves,
            2 * flops,
        )[0]
        for chunk in range(z.chunks)
    ]
    block = range_bins // sub_count
    beams = sub_count * rows
    if block % LANES or beams > MXU or sub_count < 8:
        (children,) = call(
            functools.partial(ranges_kernel, z), [shape((outer, 2, rows, LANES), f32)], backs, [mid], flops
        )
        known = (sends[-1] + arrived[-1])[2 * z.group :].reshape(-1, LANES)
        for level in range(z.last - 1):
            known = known + swapped(known, "sub", level)
        return wide_turn(z, block, children, known)

    per_block = block // LANES
    pairs = sub_count // 2
    lines = 2 * per_block * rows
    riding = z.last > 2
    messages = [(0, 1)] + [away for away in pair_order(pairs)]
    *dealt, known = call(
        functools.partial(deal_kernel, z, per_block, messages, messages.index((2, 3)) if riding else None),
        [
            shape((len(aways) * lines + tail * (riding and aways == (2, 3)), LANES), f32)
            for aways in messages
        ]
        + [shape((tail, LANES), f32)],
        [*backs, sends[-1], arrived[-1]],
        [mid, pltpu.VMEM((sub_count, lines, LANES), f32)],
        flops,
    )
    got, places = {}, {}
    for aways, message in zip(messages, dealt):
        if aways[0] > 0:
            route = [(i, i ^ aways[0]) for i in range(sub_count)]
            message = lax.ppermute(message, "sub", route)
        got[aways] = message
        places[aways[0]] = (message, 0)
    early = [k for k in range(pairs) if k // 2 % 2 == 0]
    late = [k for k in range(pairs) if k // 2 % 2]
    blend, partial = None, []
    for cut in (early, late):
        swaps = [(2 * k, 2 * k + 1) for k in cut if (2 * k, 2 * k + 1) in got]
        records = [known] + [got[2, 3]] * riding if cut is early else []
        (both,) = call(
            functools.partial(stack_kernel, lines, len(swaps)),
            [shape((len(swaps) * lines + tail * bool(records), LANES), f32)],
            [got[pair] for pair in swaps] + records,
            [],
            1,
        )
        crossed = swapped(both, "sub", 0)
        places.update({pair[1]: (crossed, i * lines) for i, pair in enumerate(swaps)})
        order = [2 * k + side for k in cut for side in range(2)]
        if cut is early:
            blend = call(
                functools.partial(last_blend_kernel, z, order + [2 * k + side for k in late for side in range(2)]),
                [shape((beams, beams), bf16)] * 2,
                [both, crossed],
                [],
                1 << 18,
            )
        arrays = []
        spots = []
        for away in order:
            array, at = places[away]
            index = [i for i, other in enumerate(arrays) if other is array]
            if not index:
                index = [len(arrays)]
                arrays.append(array)
            spots.append((index[0], at))
        partial = call(
            functools.partial(turn_kernel, z, per_block, spots, 0 if cut is early else len(order) * rows, len(partial)),
            [shape((2, block, beams), f32)],
            [*arrays, *blend, *partial],
            [pltpu.VMEM((2, block, beams), f32), pltpu.SemaphoreType.DMA((2 * per_block,))] * len(partial),
            flops,
            out_space=pltpu.HBM if partial else pltpu.VMEM,
        )
    return partial[0]


def wide_turn(z, block, children, known):
    sub_count, rows, half = z.sub_count, z.rows, z.half
    if block % LANES == 0:
        line = children.reshape(sub_count, block // LANES, 2, rows, LANES).transpose(0, 2, 3, 1, 4)
    else:
        line = children.reshape(z.outer, 2, rows, LANES // block, block).transpose(0, 3, 1, 2, 4)
    gathered = lax.all_to_all(line.reshape(sub_count, 2 * rows, block), "sub", 0, 0, tiled=True)
    gathered = gathered.reshape(sub_count, 2, 2, half, block)
    table = known.reshape(z.blocks, z.record, z.slots, rows).transpose(0, 2, 1, 3)
    table = table.reshape(-1, z.record, rows)[:sub_count]
    weights = table[:, : z.at_offset].reshape(sub_count, 2, z.taps, rows)
    offsets = table[:, z.at_offset : z.at_shift].astype(jnp.int32)
    columns = jnp.arange(half, dtype=jnp.int32)
    stencil = 0.0
    for tap in range(z.taps):
        hits = columns == offsets[..., None] + tap
        stencil = stencil + jnp.where(hits, weights[:, :, tap, :, None], 0.0)
    index = jnp.arange(sub_count, dtype=jnp.int32)
    side = (index >> z.last & 1)[:, None, None, None]
    chosen = jnp.where(side == 0, gathered[:, :, 0], gathered[:, :, 1])
    crossing = gathered[index ^ (1 << z.last)]
    crossing = jnp.where(side == 0, crossing[:, :, 0], crossing[:, :, 1])
    both = jnp.concatenate([chosen, crossing], axis=2)
    matrix = jnp.moveaxis(stencil, 1, 2).reshape(sub_count, rows, rows)
    merged = jnp.einsum("ijm,ipmq->pqij", matrix, both, precision=lax.Precision.HIGHEST)
    return merged.reshape(2, block, sub_count * rows)


def solution(mesh):
    placed = (
        P(None, ("img", "sub"), None),
        P(None, "sub", None, None),
        P(None, "sub", None, None),
        P(None, "sub", None, None),
        P(None, "sub", None, None, None),
    )

    return jax.shard_map(body, mesh=mesh, in_specs=placed, out_specs=P(None, ("img", "sub"), None), check_vma=False)
```

```python
import functools
import math

import jax
import jax.numpy as jnp
import numpy as np
from jax import lax
from jax.experimental import pallas as pl
from jax.experimental.pallas import tpu as pltpu
from jax.sharding import PartitionSpec as P


LANES = 128
MXU = 256
CHUNK = 256
VMEM_GRANT = 12 << 20
f32 = jnp.float32
bf16 = jnp.bfloat16


def swapped(block, axis, stride):
    count = lax.axis_size(axis)
    route = []
    for low in range(count):
        high = low | 1 << stride
        if high != low and high < count:
            route += [(low, high), (high, low)]
    return lax.ppermute(block, axis, route)


def call(kernel, outs, ins, scratch, flops, space=pltpu.VMEM, out_space=pltpu.VMEM):
    moved = sum(math.prod(o.shape) * o.dtype.itemsize for o in outs)
    moved += sum(math.prod(i.shape) * i.dtype.itemsize for i in ins)
    return pl.pallas_call(
        kernel,
        out_shape=outs,
        in_specs=[pl.BlockSpec(memory_space=space)] * len(ins),
        out_specs=[pl.BlockSpec(memory_space=out_space)] * len(outs),
        scratch_shapes=scratch,
        cost_estimate=pl.CostEstimate(flops=flops, bytes_accessed=moved, transcendentals=0),
        compiler_params=pltpu.CompilerParams(vmem_limit_bytes=VMEM_GRANT),
    )(*ins)


def lane_matrix(direction, scale):
    k = np.arange(LANES)
    angle = direction * 2.0 * np.pi * (np.outer(k, k) % LANES) / LANES
    c, s = np.cos(angle) * scale, np.sin(angle) * scale
    full = np.block([[c, s], [-s, c]]).astype(np.float32)
    high = full.astype(bf16)
    low = (full - high.astype(np.float32)).astype(bf16)
    return high, low


def lane_twiddle(outer, direction):
    total = outer * LANES
    turns = np.outer(np.arange(outer), np.arange(LANES)) % total
    angle = direction * 2.0 * np.pi * turns / total
    return np.stack([np.cos(angle), np.sin(angle)]).astype(np.float32)


def times_constant(value, turn):
    real, imag = value
    turn = turn % 1.0
    if turn == 0.0:
        return value
    if turn == 0.5:
        return (-real, -imag)
    if turn == 0.25:
        return (-imag, real)
    if turn == 0.75:
        return (imag, -real)
    c, s = math.cos(2 * math.pi * turn), math.sin(2 * math.pi * turn)
    if abs(abs(c) - abs(s)) < 1e-12:
        r = abs(c)
        sc, ss = math.copysign(1, c), math.copysign(1, s)
        a = (real if sc > 0 else -real) - (imag if ss > 0 else -imag)
        b = (real if ss > 0 else -real) + (imag if sc > 0 else -imag)
        return (a * r, b * r)
    return (real * c - imag * s, real * s + imag * c)


def small_dft(values, direction):
    count = len(values)
    if count == 1:
        return values
    even = small_dft(values[0::2], direction)
    odd = small_dft(values[1::2], direction)
    first, second = [], []
    for k in range(count // 2):
        o = times_constant(odd[k], direction * k / count)
        e = even[k]
        first.append((e[0] + o[0], e[1] + o[1]))
        second.append((e[0] - o[0], e[1] - o[1]))
    return first + second


def split_factors(count):
    inner = 1 << ((count.bit_length() - 1) + 1) // 2
    return count // inner, inner


def staged_dft(count, direction, load, store, scratch):
    outer, inner = split_factors(count)
    for b in range(inner):
        got = small_dft([load(inner * a + b) for a in range(outer)], direction)
        for c in range(outer):
            value = times_constant(got[c], direction * b * c / count)
            scratch[0, c * inner + b] = value[0]
            scratch[1, c * inner + b] = value[1]
    for c in range(outer):
        line = [(scratch[0, c * inner + b], scratch[1, c * inner + b]) for b in range(inner)]
        got = small_dft(line, direction)
        for d in range(inner):
            store(c + outer * d, got[d])


def put_split(high_ref, low_ref, row, rows, value):
    for part in range(2):
        high = value[part].astype(bf16)
        low = (value[part] - high.astype(f32)).astype(bf16)
        high_ref[row : row + rows, part * LANES : (part + 1) * LANES] = high
        low_ref[row : row + rows, part * LANES : (part + 1) * LANES] = low


def dot3(left_high, left_low, right_high, right_low):
    def one(a, b):
        return jnp.dot(a, b, preferred_element_type=f32)

    return one(left_high, right_high) + (one(left_low, right_high) + one(left_high, right_low))


def put_halves(keep_ref, send_ref, bit, group, i, block, half):
    low, high = block[:half], block[half:]
    keep = jnp.where(bit == 0, low, high)
    send = jnp.where(bit == 0, high, low)
    for part in range(2):
        cut = slice(part * LANES, (part + 1) * LANES)
        keep_ref[part * group + i] = keep[:, cut]
        send_ref[part * group + i] = send[:, cut]


def cos_sin(turns, full):
    quarter = full // 4
    turns = turns & (full - 1)
    quadrant = (turns + quarter // 2) >> (quarter.bit_length() - 1)
    x = (turns - quadrant * quarter).astype(f32) * (2.0 * math.pi / full)
    y = x * x
    sine, cosine = 0.0, 0.0
    for term in (9, 7, 5, 3, 1):
        sine = sine * y + (-1.0) ** (term // 2) / math.factorial(term)
    for term in (10, 8, 6, 4, 2, 0):
        cosine = cosine * y + (-1.0) ** (term // 2) / math.factorial(term)
    sine = sine * x
    odd = (quadrant & 1) == 1
    first = jnp.where(odd, sine, cosine)
    second = jnp.where(odd, cosine, sine)
    first = jnp.where(((quadrant + 1) & 2) == 2, -first, first)
    return first, jnp.where((quadrant & 2) == 2, -second, second)


class Sizes:
    def __init__(self, rows, outer, taps, sub_count):
        self.rows, self.outer, self.taps, self.sub_count = rows, outer, taps, sub_count
        self.half = rows // 2
        self.levels = sub_count.bit_length() - 1
        self.last = self.levels - 1
        self.group = max(1, min(outer, CHUNK // rows))
        self.at_offset = 2 * taps
        self.at_shift = self.at_offset + 2
        self.at_phase = self.at_shift + 2
        self.record = -(-(self.at_phase + 2) // 8) * 8
        self.pages = -(-self.levels * self.record // LANES)
        self.slots = LANES // rows
        self.blocks = -(-sub_count // self.slots)
        self.chunks = outer // self.group
        self.last_page = self.last * self.record // LANES


def prepare(z, shift, phase, offset, weight, tabs, pack, lines):
    me = lax.axis_index("sub")
    lines[...] = jnp.zeros_like(lines)
    for level in range(z.levels):
        at = level * z.record
        for c in range(2):
            lines[at + c * z.taps : at + (c + 1) * z.taps, : z.rows] = weight[level, 0, c]
        at += z.at_offset
        lines[at : at + 2, : z.rows] = offset[level, 0].astype(f32)
        lines[at + 2 : at + 4, : z.half] = shift[level, 0].astype(f32)
        lines[at + 4 : at + 6, : z.half] = phase[level, 0]
    for page in range(z.pages):
        turned = lines[page * LANES : (page + 1) * LANES, :].T[: z.rows]
        tabs[:, page * LANES : (page + 1) * LANES] = turned
        if page == z.last_page:
            pack[: z.rows] = turned
    spread = lines[z.last * z.record : (z.last + 1) * z.record, :]
    step = z.rows
    while step < LANES:
        spread = spread + pltpu.roll(spread, step, 1)
        step *= 2
    slot = lax.broadcasted_iota(jnp.int32, spread.shape, 1) // z.rows
    for block in range(z.blocks):
        at = z.rows + block * z.record
        pack[at : at + z.record] = jnp.where(slot + block * z.slots == me, spread, 0.0)


def rotation(z, shifts, phases, near, far):
    full = 4 * z.outer * LANES
    shape = (z.rows, LANES)
    lane = lax.broadcasted_iota(jnp.int32, shape, 1)
    signed = z.outer * jnp.where(lane >= LANES // 2, lane - LANES, lane)
    shifts = jnp.broadcast_to(jnp.concatenate(shifts, axis=0), shape).astype(jnp.int32)
    phases = jnp.broadcast_to(jnp.concatenate(phases, axis=0), shape)
    c, s = cos_sin(shifts * signed, full)
    pc, ps = jnp.cos(phases), jnp.sin(phases)
    near[0] = pc * c + ps * s
    near[1] = ps * c - pc * s
    c, s = cos_sin(shifts * lane, full)
    far[0] = c
    far[1] = -s


def of_children(z, table, at):
    return [table[: z.half, at + c : at + c + 1] for c in range(2)]


def last_tables_kernel(z, pack, other, near, far):
    low = (lax.axis_index("sub") >> z.last & 1) == 0
    at = z.last * z.record - z.last_page * LANES
    both = []
    for row in (z.at_shift, z.at_phase):
        mine = of_children(z, pack, at + row)[0]
        their = of_children(z, other, at + row)[1]
        both.append([jnp.where(low, mine, their), jnp.where(low, their, mine)])
    rotation(z, *both, near, far)


def tables_kernel(z, tabs, near, far, wide_high, wide_low):
    for level in range(z.last):
        at = level * z.record
        shifts, phases = of_children(z, tabs, at + z.at_shift), of_children(z, tabs, at + z.at_phase)
        rotation(z, shifts, phases, near.at[level], far.at[level])
    size = z.group * z.rows
    shape = (z.rows, size)
    column = lax.broadcasted_iota(jnp.int32, shape, 1)
    beam = column % z.half
    child = (column // z.half) % 2
    block = column // z.rows
    for level in range(z.last):
        at = level * z.record
        wide = jnp.zeros(shape, f32)
        for c in range(2):
            first = tabs[:, at + z.at_offset + c : at + z.at_offset + c + 1].astype(jnp.int32)
            for tap in range(z.taps):
                hits = (beam == first + tap) & (child == c)
                wide += jnp.where(hits, tabs[:, at + c * z.taps + tap : at + c * z.taps + tap + 1], 0.0)
        for i in range(z.group):
            value = jnp.where(block == i, wide, 0.0)
            high = value.astype(bf16)
            wide_high[level, i * z.rows : (i + 1) * z.rows] = high
            wide_low[level, i * z.rows : (i + 1) * z.rows] = (value - high.astype(f32)).astype(bf16)


def last_blend_kernel(z, order, ours, theirs, blend_high, blend_low):
    tail = z.blocks * z.record
    known = ours[ours.shape[0] - tail :] + theirs[theirs.shape[0] - tail :]
    me = lax.axis_index("sub")
    beams = z.sub_count * z.rows
    for block in range(beams // LANES):
        table = known[block * z.record : (block + 1) * z.record]
        shape = (z.rows, LANES)
        row = lax.broadcasted_iota(jnp.int32, shape, 0)
        owner = lax.broadcasted_iota(jnp.int32, shape, 1) // z.rows + block * z.slots
        mine = (row // z.half) == (owner >> z.last & 1)
        parts = []
        for c in range(2):
            first = jnp.broadcast_to(table[z.at_offset + c : z.at_offset + c + 1].astype(jnp.int32), shape)
            total = jnp.zeros(shape, f32)
            for tap in range(z.taps):
                hits = (row % z.half == first + tap) & mine
                line = jnp.broadcast_to(table[c * z.taps + tap : c * z.taps + tap + 1], shape)
                total += jnp.where(hits, line, 0.0)
            parts.append(total)
        for i, away in enumerate(order):
            source = me ^ away
            value = jnp.where(owner == source, parts[0], 0.0)
            value = jnp.where(owner == (source ^ (1 << z.last)), parts[1], value)
            high = value.astype(bf16)
            at = (slice(i * z.rows, (i + 1) * z.rows), slice(block * LANES, (block + 1) * LANES))
            blend_high[at] = high
            blend_low[at] = (value - high.astype(f32)).astype(bf16)


def forward(z, load, keep, mid, high, low, high_m, low_m, twiddle):
    held = []

    def store(k, value):
        c, s = twiddle[0, k : k + 1, :], twiddle[1, k : k + 1, :]
        held.append((k, (value[0] * c - value[1] * s, value[0] * s + value[1] * c)))
        if len(held) % 2 == 0:
            pair = tuple(jnp.concatenate([held[-2][1][p], held[-1][1][p]], axis=0) for p in range(2))
            put_split(high, low, (len(held) - 2) * z.half, 2 * z.half, pair)

    staged_dft(z.outer, -1, load, store, mid)
    out = dot3(high[...], low[...], high_m, low_m)
    for i, (k, _) in enumerate(held):
        for part in range(2):
            keep[part * z.outer + k] = out[i * z.half : (i + 1) * z.half, part * LANES : (part + 1) * LANES]


def start_kernel(z, *refs):
    sources, refs = refs[:8], refs[8:]
    tabs, pack, keep, refs = refs[0], refs[1], refs[2], refs[3:]
    held, (lines, mid, high, low, sems) = refs[:8], refs[8:]
    bit = lax.axis_index("sub") & 1
    rows = pl.ds(pl.multiple_of(bit * z.half, z.half), z.half)
    sources = [*sources[:4], sources[4].at[:, rows], *sources[5:]]
    copies = [
        pltpu.make_async_copy(source, place, sems.at[i])
        for i, (source, place) in enumerate(zip(sources, held))
    ]
    for copy in copies:
        copy.start()
    for copy in copies[:4]:
        copy.wait()
    prepare(z, *held[:4], tabs, pack, lines)
    image, twiddle, high_m, low_m = held[4:]
    for copy in copies[4:]:
        copy.wait()

    def load(q):
        cut = slice(q * LANES, (q + 1) * LANES)
        return image[0, :, cut], image[1, :, cut]

    forward(z, load, keep, mid, high, low, high_m[...], low_m[...], twiddle)


def join_kernel(z, image, twiddle, high_m, low_m, kept, near, far, wide_high, wide_low, keep, send, spectrum, mid, high, low):
    bit = lax.axis_index("sub") & 1
    rows = pl.ds(pl.multiple_of(bit * z.half, z.half), z.half)

    def load(q):
        cut = slice(q * LANES, (q + 1) * LANES)
        return image[0, rows, cut], image[1, rows, cut]

    forward(z, load, spectrum, mid, high, low, high_m[...], low_m[...], twiddle)
    level_kernel(z, 0, 0, 0, z.outer, kept, spectrum, near, far, wide_high, wide_low, keep, send, high, low)


def rotated(value, near, far, k):
    shape = value[0].shape
    fr = jnp.broadcast_to(far[0][:, k : k + 1], shape)
    fi = jnp.broadcast_to(far[1][:, k : k + 1], shape)
    nr, ni = near[0], near[1]
    rr, ri = nr * fr - ni * fi, nr * fi + ni * fr
    return value[0] * rr - value[1] * ri, value[0] * ri + value[1] * rr


def blended(z, level, chunk, stride, keep, arrived, near, far, wide_high, wide_low, high, low):
    close = near[level, 0], near[level, 1]
    steps = far[level, 0], far[level, 1]
    for i in range(z.group):
        spots = [part * z.group + i for part in range(2)]
        if stride:
            spots = [part * stride + chunk * z.group + i for part in range(2)]
        value = tuple(jnp.concatenate([keep[spot], arrived[spot]], axis=0) for spot in spots)
        value = rotated(value, close, steps, chunk * z.group + i)
        put_split(high, low, i * z.rows, z.rows, value)
    return dot3(wide_high[level], wide_low[level], high[...], low[...])


def level_kernel(z, level, chunk, riding, stride, kept, arrived, *refs):
    packs, refs = refs[:riding], refs[riding:]
    near, far, wide_high, wide_low, keep, send, high, low = refs
    bit = lax.axis_index("sub") >> (level + 1) & 1
    out = blended(z, level, chunk, stride, kept, arrived, near, far, wide_high, wide_low, high, low)
    for i in range(z.group):
        put_halves(keep, send, bit, z.group, i, out[i * z.rows : (i + 1) * z.rows], z.half)
    if riding:
        known = packs[0][z.rows :] + packs[1][z.rows :]
        send[2 * z.group :] = known.reshape(-1, z.half, LANES)


def return_kernel(
    z, chunk, kept, arrived, near, far, wide_high, wide_low, last_near, last_far,
    high_m, low_m, twiddle, back, high, low,
):
    out = blended(z, z.last - 1, chunk, 0, kept, arrived, near, far, wide_high, wide_low, high, low)
    close = last_near[0], last_near[1]
    steps = last_far[0], last_far[1]
    for i in range(z.group):
        block = out[i * z.rows : (i + 1) * z.rows]
        value = rotated((block[:, :LANES], block[:, LANES:]), close, steps, chunk * z.group + i)
        put_split(high, low, i * z.rows, z.rows, value)
    out = dot3(high[...], low[...], high_m[...], low_m[...])
    for i in range(z.group):
        k = chunk * z.group + i
        block = out[i * z.rows : (i + 1) * z.rows]
        real, imag = block[:, :LANES], block[:, LANES:]
        c, s = twiddle[0, k : k + 1, :], twiddle[1, k : k + 1, :]
        back[0, i] = real * c - imag * s
        back[1, i] = real * s + imag * c


def gather_back(z, backs, store, mid):
    def load(k):
        back, i = backs[k // z.group], k % z.group
        return back[0, i], back[1, i]

    staged_dft(z.outer, 1, load, store, mid)


def ranges_kernel(z, *refs):
    backs, out_ref, mid = refs[: z.chunks], refs[z.chunks], refs[z.chunks + 1]

    def store(q, value):
        for part in range(2):
            out_ref[q, part] = value[part]

    gather_back(z, backs, store, mid)


def deal_kernel(z, per_block, messages, riding, *refs):
    lines = 2 * per_block * z.rows
    backs, refs = refs[: z.chunks], refs[z.chunks :]
    sent, arrived, refs = refs[0], refs[1], refs[2:]
    outs, (records, mid, whole) = refs[: len(messages)], refs[len(messages) :]

    def store(q, value):
        for part in range(2):
            at = (part * per_block + q % per_block) * z.rows
            whole[q // per_block, at : at + z.rows] = value[part]

    gather_back(z, backs, store, mid)
    me = lax.axis_index("sub")
    for out, aways in zip(outs, messages):
        for i, away in enumerate(aways):
            out[i * lines : (i + 1) * lines] = whole[me ^ away]
    known = (sent[2 * z.group :] + arrived[2 * z.group :]).reshape(-1, LANES)
    records[...] = known
    if riding is not None:
        outs[riding][2 * lines :] = known


def stack_kernel(lines, count, *refs):
    for i, ref in enumerate(refs[:count]):
        refs[-1][i * lines : (i + 1) * lines] = ref[lines : 2 * lines]
    if len(refs) > count + 1:
        known = refs[count][...]
        for ref in refs[count + 1 : -1]:
            known = known + ref[2 * lines :]
        refs[-1][count * lines :] = known


def merge_kernel(lines, *refs):
    count = len(refs) // 2
    mine, theirs, outs = refs[:count], refs[count], refs[count + 1 :]
    for i in range(count):
        outs[i][:lines] = mine[i][...]
        outs[i][lines:] = theirs[i * lines : (i + 1) * lines]


def turn_kernel(z, per_block, places, first, adding, *refs):
    scratch = refs[len(refs) - 2 * adding :]
    refs = refs[: len(refs) - 2 * adding]
    blend_high, blend_low, *partial, out_ref = refs[len(refs) - 3 - adding :]
    size = len(places) * z.rows
    cut = slice(first, first + size)
    copies = []
    for part in range(2 * per_block):
        line = []
        for array, at in places:
            at += part * z.rows
            line.append(refs[array][at : at + z.rows])
        line = jnp.concatenate(line, axis=0).T
        high = line.astype(bf16)
        low = (line - high.astype(f32)).astype(bf16)
        total = dot3(high, low, blend_high[cut], blend_low[cut])
        at = (part // per_block, slice(part % per_block * LANES, (part % per_block + 1) * LANES))
        if adding:
            ready, sems = scratch
            ready[at] = total + partial[0][at]
            copies.append(pltpu.make_async_copy(ready.at[at], out_ref.at[at], sems.at[part]))
            copies[-1].start()
        else:
            out_ref[at] = total
    for copy in copies:
        copy.wait()


def groups(pairs):
    return [k for k in range(pairs) if k // 2 % 2 == 0], [k for k in range(pairs) if k // 2 % 2]


def pair_order(pairs):
    return [*range(pairs // 2, pairs), *range(1, pairs // 2)]


def body(sub_images, shift_table, phase_table, offset_table, weight_table):
    _, rows, range_bins = sub_images.shape
    outer = range_bins // LANES
    sub_count = lax.axis_size("sub")
    z = Sizes(rows, outer, weight_table.shape[3], sub_count)
    size = z.group * rows
    flops = 3 * 2 * size * MXU * MXU
    shape = jax.ShapeDtypeStruct
    mid = pltpu.VMEM((2, outer, rows, LANES), f32)
    halves = [pltpu.VMEM((size, 2 * LANES), bf16)] * 2
    slab = shape((2 * z.group, z.half, LANES), f32)

    def swap(send, level):
        return swapped(send, "sub", level)

    raw = swap(sub_images, 0)
    constants = [jnp.asarray(table) for table in (lane_twiddle(outer, -1), *lane_matrix(-1, 1.0))]
    sources = [shift_table, phase_table, offset_table, weight_table, sub_images, *constants]
    sources = [pltpu.with_memory_space_constraint(source, pltpu.HBM) for source in sources]
    spectra = shape((2 * outer, z.half, LANES), f32)
    small = pltpu.VMEM((2, outer, z.half, LANES), f32)
    places = [source.shape for source in sources]
    places[4] = (2, z.half, range_bins)
    tabs, pack, kept = call(
        functools.partial(start_kernel, z),
        [shape((rows, z.pages * LANES), f32), shape((rows + z.blocks * z.record, LANES), f32), spectra],
        sources,
        [pltpu.VMEM(place, source.dtype) for place, source in zip(places, sources)]
        + [pltpu.VMEM((z.pages * LANES, LANES), f32), small]
        + [pltpu.VMEM((outer * z.half, 2 * LANES), bf16)] * 2
        + [pltpu.SemaphoreType.DMA((len(sources),))],
        flops * z.chunks // 2,
        space=pltpu.HBM,
    )
    tables = call(
        functools.partial(tables_kernel, z),
        [shape((z.last, 2, rows, LANES), f32)] * 2 + [shape((z.last, size, size), bf16)] * 2,
        [tabs],
        [],
        1 << 20,
    )
    keep, send, spectrum = call(
        functools.partial(join_kernel, z),
        [slab, slab, spectra],
        [raw, *constants, kept, *tables],
        [small] + [pltpu.VMEM((outer * z.half, 2 * LANES), bf16)] * 2,
        flops * (1 + z.chunks // 2),
    )
    keeps, sends = [kept] * z.chunks, [None] * z.chunks
    arrived = [spectrum] * z.chunks
    keeps[0], sends[0], arrived[0] = keep, send, swap(send, 1)

    other = swapped(pack, "sub", z.last)
    tail = z.blocks * z.record
    longer = shape((2 * z.group + tail // z.half, z.half, LANES), f32)
    for level in range(z.last - 1):
        for chunk in range(0 if level else 1, z.chunks):
            rides = level == z.last - 2 and chunk == z.chunks - 1
            keeps[chunk], sends[chunk] = call(
                functools.partial(level_kernel, z, level, chunk, 2 * rides, 0 if level else z.outer),
                [slab, longer if rides else slab],
                [keeps[chunk], arrived[chunk]] + [pack, other] * rides + list(tables),
                halves,
                flops,
            )
            arrived[chunk] = swap(sends[chunk], level + 1)
    last_tables = call(
        functools.partial(last_tables_kernel, z),
        [shape((2, rows, LANES), f32)] * 2,
        [pack, other],
        [],
        1 << 16,
    )
    way_back = [*lane_matrix(1, 1.0 / range_bins), lane_twiddle(outer, 1)]
    backs = [
        call(
            functools.partial(return_kernel, z, chunk),
            [shape((2, z.group, rows, LANES), f32)],
            [keeps[chunk], arrived[chunk], *tables, *last_tables, *way_back],
            halves,
            2 * flops,
        )[0]
        for chunk in range(z.chunks)
    ]
    block = range_bins // sub_count
    beams = sub_count * rows
    if block % LANES or beams > MXU or sub_count < 8:
        (children,) = call(
            functools.partial(ranges_kernel, z),
            [shape((outer, 2, rows, LANES), f32)],
            backs,
            [mid],
            flops,
        )
        known = (sends[-1] + arrived[-1])[2 * z.group :].reshape(-1, LANES)
        for level in range(z.last - 1):
            known = known + swapped(known, "sub", level)
        return wide_turn(z, block, children, known)

    per_block = block // LANES
    pairs = sub_count // 2
    lines = 2 * per_block * rows
    riding = z.last > 2
    early, late = groups(pairs)
    messages = [(2 * k, 2 * k + 1) for k in early] + [(2 * k,) for k in late]
    messages.append(tuple(2 * k + 1 for k in late))
    *dealt, known = call(
        functools.partial(deal_kernel, z, per_block, messages, messages.index((2, 3)) if riding else None),
        [
            shape((len(aways) * lines + tail * (riding and aways == (2, 3)), LANES), f32)
            for aways in messages
        ]
        + [shape((tail, LANES), f32)],
        [*backs, sends[-1], arrived[-1]],
        [mid, pltpu.VMEM((sub_count, lines, LANES), f32)],
        flops,
    )
    theirs = swapped(dealt[-1], "sub", 0)
    merged = call(
        functools.partial(merge_kernel, lines),
        [shape((2 * lines, LANES), f32)] * len(late),
        [*dealt[len(early) : -1], theirs],
        [],
        1,
    )
    outgoing = dict(zip([*early, *late], [*dealt[: len(early)], *merged]))
    got = {0: outgoing[0]}
    for k in pair_order(pairs):
        route = [(i, i ^ (2 * k)) for i in range(sub_count)]
        got[k] = lax.ppermute(outgoing[k], "sub", route)
    records = [known] + [got[1]] * riding
    (both,) = call(
        functools.partial(stack_kernel, lines, len(early)),
        [shape((len(early) * lines + tail, LANES), f32)],
        [got[k] for k in early] + records,
        [],
        1,
    )
    crossed = swapped(both, "sub", 0)
    order = [2 * k + side for k in [*early, *late] for side in range(2)]
    blend = call(
        functools.partial(last_blend_kernel, z, order),
        [shape((beams, beams), bf16)] * 2,
        [both, crossed],
        [],
        1 << 18,
    )
    count = len(early)
    spots = [spot for i in range(count) for spot in ((i, 0), (count, i * lines))]
    partial = call(
        functools.partial(turn_kernel, z, per_block, spots, 0, 0),
        [shape((2, block, beams), f32)],
        [got[k] for k in early] + [crossed, *blend],
        [],
        flops,
    )
    spots = [(i, side * lines) for i in range(len(late)) for side in range(2)]
    (turned,) = call(
        functools.partial(turn_kernel, z, per_block, spots, 2 * count * rows, 1),
        [shape((2, block, beams), f32)],
        [got[k] for k in late] + [*blend, *partial],
        [pltpu.VMEM((2, block, beams), f32), pltpu.SemaphoreType.DMA((2 * per_block,))],
        flops,
        out_space=pltpu.HBM,
    )
    return turned


def wide_turn(z, block, children, known):
    sub_count, rows, half = z.sub_count, z.rows, z.half
    if block % LANES == 0:
        line = children.reshape(sub_count, block // LANES, 2, rows, LANES).transpose(0, 2, 3, 1, 4)
    else:
        line = children.reshape(z.outer, 2, rows, LANES // block, block).transpose(0, 3, 1, 2, 4)
    gathered = lax.all_to_all(line.reshape(sub_count, 2 * rows, block), "sub", 0, 0, tiled=True)
    gathered = gathered.reshape(sub_count, 2, 2, half, block)
    table = known.reshape(z.blocks, z.record, z.slots, rows).transpose(0, 2, 1, 3)
    table = table.reshape(-1, z.record, rows)[:sub_count]
    weights = table[:, : z.at_offset].reshape(sub_count, 2, z.taps, rows)
    offsets = table[:, z.at_offset : z.at_shift].astype(jnp.int32)
    columns = jnp.arange(half, dtype=jnp.int32)
    stencil = 0.0
    for tap in range(z.taps):
        hits = columns == offsets[..., None] + tap
        stencil = stencil + jnp.where(hits, weights[:, :, tap, :, None], 0.0)
    index = jnp.arange(sub_count, dtype=jnp.int32)
    side = (index >> z.last & 1)[:, None, None, None]
    chosen = jnp.where(side == 0, gathered[:, :, 0], gathered[:, :, 1])
    crossing = gathered[index ^ (1 << z.last)]
    crossing = jnp.where(side == 0, crossing[:, :, 0], crossing[:, :, 1])
    both = jnp.concatenate([chosen, crossing], axis=2)
    matrix = jnp.moveaxis(stencil, 1, 2).reshape(sub_count, rows, rows)
    merged = jnp.einsum("ijm,ipmq->pqij", matrix, both, precision=lax.Precision.HIGHEST)
    return merged.reshape(2, block, sub_count * rows)


def solution(mesh):
    placed = (
        P(None, ("img", "sub"), None),
        P(None, "sub", None, None),
        P(None, "sub", None, None),
        P(None, "sub", None, None),
        P(None, "sub", None, None, None),
    )

    return jax.shard_map(
        body, mesh=mesh, in_specs=placed, out_specs=P(None, ("img", "sub"), None), check_vma=False
    )
```
